32 devices in a mesh: face: 8 (over y, x, core), member: 4 (over z).
Axes of the slice: x: 2, y: 2, z: 4, core: 2. Of those that a mesh axis runs over, the one named last changes fastest.
Arguments:
- features: bfloat16 [8, 48, 16, 16, 256], P('member', 'face'), may hold values from -6 to 6
- observed: bfloat16 [48, 80, 256], P('face', None, 'member'), may hold values from -6 to 6
- conv_weights: bfloat16 [2304, 2, 256], P(('face', 'member')), may hold values from -0.125 to 0.125
- head_weight: bfloat16 [256, 80], P(('face', 'member')), may hold values from -0.375 to 0.375
- adjacency: int32 [48, 4, 3], replicated, may hold values from 0 to 47, as said below
- placement_map: int32 [48], replicated, may hold values from 0 to 47, each once
Outputs:
- conv_grads: float32 [2304, 2, 256], P(('face', 'member'))
- head_grad: float32 [256, 80], P(('face', 'member'))
The draws below stay inside these ranges and needn't reach their ends.
Inputs may be any that keep to these rules, and one draw needn't show every extreme that they name: `adjacency`: the table is the gluing of the 12 HEALPix base faces, each cut into 4 square tiles, under a labelling of the tiles drawn from the seed: entry [t, a] = (n, b, f) glues side a of tile t to side b of tile n, reversed when f is 1; the gluing is mutual (entry [n, b] is (t, a, f)) and never joins a side to itself. `placement_map`: each tile stands at exactly one slot.
All inputs are finite; a program needn't handle non-finite values.
Results may differ from the reference program's by a relative error of at most 0.0005.
Values may be sent and summed in bfloat16 or wider, within the bound.
A program may use at most 128 MiB of HBM per device.

```python
import math
import jax
import jax.numpy as jnp
import numpy as np
from jax import lax

C = 256
VARS = 80
FACES = 12
TILES_FACE = 4
TILE = 16
MEMBERS = 8
TILE_TOTAL = 48


def face_gluing(face, side):
    cycle, pos = divmod(face, 4)
    if cycle == 0:
        table = [((pos - 1) % 4, 1, 1), ((pos + 1) % 4, 0, 1), (4 + (pos + 1) % 4, 0, 0), (4 + pos, 1, 0)]
    elif cycle == 1:
        table = [((pos - 1) % 4, 2, 0), (pos, 3, 0), (8 + pos, 0, 0), (8 + (pos - 1) % 4, 1, 0)]
    else:
        table = [(4 + pos, 2, 0), (4 + (pos + 1) % 4, 3, 0), (8 + (pos + 1) % 4, 3, 1), (8 + (pos - 1) % 4, 2, 1)]
    return table[side]


def tile_on_side(side, place, width):
    if side == 0:
        return (0, place)
    if side == 1:
        return (place, width - 1)
    if side == 2:
        return (width - 1, place)
    return (place, 0)


def canonical_table():
    width = math.isqrt(TILES_FACE)
    rows_out = []
    for face in range(FACES):
        for tile_row in range(width):
            for tile_col in range(width):
                base = face * width * width
                entry = []
                for side in range(4):
                    inside = [tile_row > 0, tile_col < width - 1, tile_row < width - 1, tile_col > 0][side]
                    if inside:
                        step_row = [-1, 0, 1, 0][side]
                        step_col = [0, 1, 0, -1][side]
                        entry.append([base + (tile_row + step_row) * width + tile_col + step_col, (side + 2) % 4, 0])
                    else:
                        place = tile_col if side in (0, 2) else tile_row
                        other_face, other_side, flip_bit = face_gluing(face, side)
                        if flip_bit == 1:
                            place = width - 1 - place
                        other_row, other_col = tile_on_side(other_side, place, width)
                        entry.append([other_face * width * width + other_row * width + other_col, other_side, flip_bit])
                rows_out.append(entry)
    return np.array(rows_out, dtype=np.int32)


def draw_adjacency(key, part):
    canonical_order = jnp.asarray(canonical_table())
    label_list = jax.random.permutation(jax.random.fold_in(key, 11), TILE_TOTAL).astype(jnp.int32)
    renumbered_labels = jnp.stack([label_list[canonical_order[:, :, 0]], canonical_order[:, :, 1], canonical_order[:, :, 2]], axis=-1).astype(jnp.int32)
    return jnp.zeros((TILE_TOTAL, 4, 3), jnp.int32).at[label_list].set(renumbered_labels)


def with_spikes(values, stream_key, source, target, shards_of, factor):
    owner, partner = [(jnp.arange(values.shape[axis_at]) // (values.shape[axis_at] // shards_of)).reshape([-1 if axis == axis_at else 1 for axis in range(values.ndim)]) for axis_at in (source, target)]
    chosen = jax.random.permutation(stream_key, shards_of)[partner]
    strong = (owner == chosen) | (owner == (partner + shards_of // 2) % shards_of)
    return jnp.where(strong, factor * values, values)


def levels(own_key, shape, pieces, least, largest):
    factor_of = 1.0
    for dim, parts in pieces:
        heights = jax.random.uniform(jax.random.fold_in(jax.random.fold_in(own_key, 6), dim), (parts,), jnp.float32, least / len(pieces), largest / len(pieces))
        factor_of = factor_of * jnp.repeat(jnp.exp(heights), shape[dim] // parts).reshape((-1,) + (1,) * (len(shape) - 1 - dim))
    return factor_of


def bell_draw(rng, extent, scale, reach, pieces=(), held_as=jnp.bfloat16):
    values = scale * jax.random.normal(rng, extent, jnp.float32)
    if pieces:
        values = values * levels(rng, extent, pieces, -0.22, 0.18)
    return jnp.clip(values, -reach, reach).astype(held_as)


def heavy_noise(own_key, dims, deviation, most, shards, heavy, kind=jnp.bfloat16):
    values = deviation * jax.random.normal(own_key, dims, jnp.float32)
    if shards:
        values = values * levels(own_key, dims, shards, -0.22, 0.18)
    return jnp.clip(with_spikes(values, jax.random.fold_in(own_key, 3), *heavy), -most, most).astype(kind)


def setup_inputs(seed: int = 0) -> dict:
    splits = jax.random.split(jax.random.key(seed), 7)
    features = heavy_noise(splits[0], (MEMBERS, TILE_TOTAL, TILE, TILE, C), 1.0, 6.0, ((0, 4), (1, 8)), (1, 4, 8, 2.0))
    observed = bell_draw(splits[1], (TILE_TOTAL, VARS, TILE * TILE), 1.0, 6.0, ((0, 8), (2, 4)))
    conv_weights = bell_draw(splits[2], (9 * C, 2, C), (9 * C) ** -0.5, 0.125, ((0, 32),))
    head_weight = bell_draw(splits[3], (C, VARS), C ** -0.5, 0.375, ((0, 32),))
    adjacency = draw_adjacency(jax.random.fold_in(splits[6], 71), 0)
    placement_map = jax.random.permutation(splits[5], TILE_TOTAL).astype(jnp.int32)
    return {"features": features, "observed": observed, "conv_weights": conv_weights, "head_weight": head_weight, "adjacency": adjacency, "placement_map": placement_map}


smooth_sq = 0.0625

def split_edges(grid_field):
    return jnp.stack([grid_field[:, :, 0], grid_field[:, :, :, -1], grid_field[:, :, -1], grid_field[:, :, :, 0]], axis=2)

def border_of(padded):
    return jnp.stack([padded[:, :, 0, 1:-1], padded[:, :, 1:-1, -1], padded[:, :, -1, 1:-1], padded[:, :, 1:-1, 0]], axis=2)

def surround(grid_field, border):
    ensemble_members, tile_count, height, tile_w, channels = grid_field.shape
    corner = jnp.zeros((ensemble_members, tile_count, 1, 1, channels), grid_field.dtype)
    top_row = jnp.concatenate([corner, border[:, :, 0][:, :, None], corner], axis=3)
    low_row = jnp.concatenate([corner, border[:, :, 2][:, :, None], corner], axis=3)
    middle = jnp.concatenate([border[:, :, 3][:, :, :, None], grid_field, border[:, :, 1][:, :, :, None]], axis=3)
    return jnp.concatenate([top_row, middle, low_row], axis=2)

def convolve(padded, weight):
    channels = weight.shape[1]
    height = padded.shape[2] - 2
    tile_w = padded.shape[3] - 2
    summed = None
    for tap_index in range(9):
        row_off, col_off = divmod(tap_index, 3)
        window = padded[:, :, row_off:row_off + height, col_off:col_off + tile_w, :]
        product_part = jnp.dot(window.reshape(-1, channels), weight[tap_index * channels:(tap_index + 1) * channels], preferred_element_type=jnp.float32)
        summed = product_part if summed is None else summed + product_part
    return summed.reshape(padded.shape[:2] + (height, tile_w, channels))

def transpose_conv(slope_in, weight):
    channels = weight.shape[1]
    ensemble_members, tile_count, height, tile_w, _ = slope_in.shape
    result = jnp.zeros((ensemble_members, tile_count, height + 2, tile_w + 2, channels), jnp.float32)
    flat_slope = slope_in.reshape(-1, channels)
    for tap_index in range(9):
        row_off, col_off = divmod(tap_index, 3)
        product_part = lax.dot_general(flat_slope, weight[tap_index * channels:(tap_index + 1) * channels], (((1,), (1,)), ((), ())), preferred_element_type=jnp.float32)
        result = result.at[:, :, row_off:row_off + height, col_off:col_off + tile_w, :].add(product_part.reshape(slope_in.shape))
    return result

def weight_slope(padded, slope_in):
    channels = slope_in.shape[-1]
    height = slope_in.shape[2]
    tile_w = slope_in.shape[3]
    flat_slope = slope_in.reshape(-1, channels)
    pieces_out = []
    for tap_index in range(9):
        row_off, col_off = divmod(tap_index, 3)
        window = padded[:, :, row_off:row_off + height, col_off:col_off + tile_w, :]
        pieces_out.append(lax.dot_general(window.reshape(-1, channels), flat_slope, (((0,), (0,)), ((), ())), preferred_element_type=jnp.float32))
    return jnp.concatenate(pieces_out, axis=0)

def dsilu(argument):
    sigmoid_v = jax.nn.sigmoid(argument)
    return sigmoid_v * (1.0 + argument * (1.0 - sigmoid_v))

def reference(features, observed, conv_weights, head_weight, adjacency, placement_map):
    ensemble_members, tile_count, height, tile_w, channels = features.shape
    slot_ids = jnp.arange(tile_count, dtype=jnp.int32)
    slot_of = lax.optimization_barrier(jnp.sum(slot_ids[:, None] * (placement_map[:, None] == slot_ids[None, :]).astype(jnp.int32), axis=0))
    entries = adjacency[placement_map]
    source_slot = slot_of[entries[:, :, 0]]
    source_side = entries[:, :, 1]
    flip_flags = entries[:, :, 2]

    def partner_borders(edges):
        picked = edges[:, source_slot, source_side]
        return jnp.where(flip_flags[None, :, :, None, None] == 1, picked[:, :, :, ::-1, :], picked)
    pad_in = surround(features, partner_borders(split_edges(features)))
    pre_one = convolve(pad_in, conv_weights[:, 0, :])
    act_one = jax.nn.silu(pre_one).astype(jnp.bfloat16)
    pad_mid = surround(act_one, partner_borders(split_edges(act_one)))
    pre_two = convolve(pad_mid, conv_weights[:, 1, :])
    act_two = jax.nn.silu(pre_two).astype(jnp.bfloat16)
    flat_two = act_two.reshape(ensemble_members, tile_count, height * tile_w, channels).astype(jnp.float32)
    outputs = jnp.einsum('mtpc,cv->mtvp', flat_two, head_weight.astype(jnp.float32)).astype(jnp.bfloat16)
    out_vals = outputs.astype(jnp.float32)
    obs_vals = observed.astype(jnp.float32)
    paired = jnp.zeros(out_vals.shape, jnp.float32)
    for column_j in range(ensemble_members):
        spread = out_vals - out_vals[column_j]
        paired = paired + spread * lax.rsqrt(spread * spread + smooth_sq)
    own_gap = out_vals - obs_vals[None]
    slope_out = ((own_gap * lax.rsqrt(own_gap * own_gap + smooth_sq) / ensemble_members - paired / (ensemble_members * ensemble_members)) / TILE).astype(jnp.bfloat16)
    slope_f = slope_out.astype(jnp.float32)
    head_grad = jnp.einsum('mtpc,mtvp->cv', flat_two, slope_f)
    back_two = jnp.einsum('mtvp,cv->mtpc', slope_f, head_weight.astype(jnp.float32)).reshape(ensemble_members, tile_count, height, tile_w, channels)
    slope_two = (back_two * dsilu(pre_two)).astype(jnp.bfloat16)
    grad_two = weight_slope(pad_mid, slope_two)
    pad_slope = transpose_conv(slope_two, conv_weights[:, 1, :]).astype(jnp.bfloat16)
    returned = partner_borders(border_of(pad_slope)).astype(jnp.float32)
    slope_mid = pad_slope[:, :, 1:-1, 1:-1].astype(jnp.float32)
    slope_mid = slope_mid.at[:, :, 0].add(returned[:, :, 0])
    slope_mid = slope_mid.at[:, :, :, -1].add(returned[:, :, 1])
    slope_mid = slope_mid.at[:, :, -1].add(returned[:, :, 2])
    slope_mid = slope_mid.at[:, :, :, 0].add(returned[:, :, 3])
    slope_one = (slope_mid * dsilu(pre_one)).astype(jnp.bfloat16)
    grad_one = weight_slope(pad_in, slope_one)
    return (jnp.stack([grad_one, grad_two], axis=1), head_grad)
```

```python
import functools

import jax
import jax.numpy as jnp
from jax import lax
from jax.experimental import pallas as pl
from jax.experimental.pallas import tpu as pltpu
from jax.sharding import PartitionSpec as P

smooth_sq = 0.0625
MESH = pl.DeviceIdType.MESH
VMEM = pltpu.VMEM
SMEM = pltpu.SMEM
f32 = jnp.float32
bf16 = jnp.bfloat16
i16 = jnp.int16
LIMIT = 62 * 1024 * 1024
TOP = 32767.0
NT = (((1,), (1,)), ((), ()))
TN = (((0,), (0,)), ((), ()))
NN = (((1,), (0,)), ((), ()))


def mm(a, b, dims=NN):
    return lax.dot_general(a, b, dims, preferred_element_type=f32)


def rcopy(src, dst, send, recv, **where):
    return pltpu.make_async_remote_copy(
        src_ref=src, dst_ref=dst, send_sem=send, recv_sem=recv, device_id=where, device_id_type=MESH
    )


def greet(chips, members):
    face = lax.axis_index("face")
    member = lax.axis_index("member")
    core = face % 2
    chip = face // 2
    barrier = pltpu.get_barrier_semaphore()
    pl.semaphore_signal(
        barrier, inc=1, device_id={"face": chip * 2 + 1 - core}, device_id_type=MESH
    )
    for j in range(1, chips):
        pl.semaphore_signal(
            barrier,
            inc=1,
            device_id={"face": ((chip + j) % chips) * 2 + core},
            device_id_type=MESH,
        )
    for j in range(1, members):
        pl.semaphore_signal(
            barrier, inc=1, device_id={"member": (member + j) % members}, device_id_type=MESH
        )
    pl.semaphore_wait(barrier, chips + members - 1)


class FaceGather:
    def __init__(self, at, chips, sems):
        self.at, self.chips, self.sems = at, chips, sems
        face = lax.axis_index("face")
        self.face, self.core, self.chip = face, face % 2, face // 2
        self.partner = self.chip * 2 + 1 - self.core

    def direct(self, j):
        mine = self.at(self.face, None)
        return rcopy(
            mine,
            mine,
            self.sems.at[0, j],
            self.sems.at[1, j],
            face=((self.chip + j) % self.chips) * 2 + self.core,
        )

    def forward(self, j):
        block = self.at(((self.chip + self.chips - j) % self.chips) * 2 + self.core, None)
        return rcopy(block, block, self.sems.at[2, j], self.sems.at[3, j], face=self.partner)

    def start(self):
        for j in range(1, self.chips):
            self.direct(j).start()
        self.forward(0).start()

    def relay_first(self):
        pass

    def relay_rest(self):
        for j in range(1, self.chips):
            self.direct(j).wait_recv()
            self.forward(j).start()

    def finish(self):
        for j in range(1, self.chips):
            self.direct(j).wait_send()
        for j in range(self.chips):
            self.forward(j).wait()


class SquareGather:
    def __init__(self, at, chips, sems):
        self.at, self.sems = at, sems
        face = lax.axis_index("face")
        core, chip = face % 2, face // 2
        col, row = chip % 2, chip // 2
        self.face = face
        self.partner = chip * 2 + 1 - core
        self.beside = (row * 2 + 1 - col) * 2 + core
        self.below = ((1 - row) * 2 + col) * 2 + core
        self.across = ((1 - row) * 2 + 1 - col) * 2 + core

    def direct(self, k):
        to = (self.beside, self.beside, self.below, self.below, self.below, self.beside)[k]
        block = (self.face,) * 4 + (self.beside, self.below)
        ref = self.at(block[k], (0, 1, 1, 0, 0, 1)[k])
        return rcopy(ref, ref, self.sems.at[0, k], self.sems.at[1, k], face=to)

    def forward(self, k):
        if k == 6:
            ref = self.at(self.face, None)
        else:
            block = (
                self.beside,
                self.beside,
                self.below,
                self.below,
                self.across,
                self.across,
            )
            ref = self.at(block[k], (0, 1, 1, 0, 0, 1)[k])
        return rcopy(ref, ref, self.sems.at[2, k], self.sems.at[3, k], face=self.partner)

    def start(self):
        for k in (0, 2, 1, 3):
            self.direct(k).start()
        self.forward(6).start()

    def relay_first(self):
        for k, onward in ((0, 4), (2, 5)):
            self.direct(k).wait_recv()
            self.direct(onward).start()
            self.forward(k).start()

    def relay_rest(self):
        for k in (1, 3, 4, 5):
            self.direct(k).wait_recv()
            self.forward(k).start()

    def finish(self):
        for k in range(6):
            self.direct(k).wait_send()
        for k in range(7):
            self.forward(k).wait()


def units(ref, rows, start, count):
    if len(ref.shape) == 3:
        return ref.at[pl.ds(start, count)] if count > 1 else ref.at[start]
    return ref.at[pl.ds(pl.multiple_of(start * rows, rows), count * rows)]


def gather_rows(ref, rows, members, chips, sems):
    def at(block, part):
        if part is None:
            return units(ref, rows, block * members, members)
        half = members // 2
        return units(ref, rows, block * members + part * half, half)

    return (SquareGather if chips == 4 and members % 2 == 0 else FaceGather)(at, chips, sems)


def gather_edges(ref, start, count, chips, sems):
    def at(block, part):
        if part is None:
            return ref.at[block, pl.ds(start, count)]
        half = count // 2
        return ref.at[block, pl.ds(start + part * half, half)]

    return (SquareGather if chips == 4 and count % 2 == 0 else FaceGather)(at, chips, sems)


class LineGather:
    def __init__(self, src, ref, rows, members, sems):
        self.src, self.ref, self.rows, self.members, self.sems = src, ref, rows, members, sems
        self.face, self.member = lax.axis_index("face"), lax.axis_index("member")

    def at(self, member):
        return units(self.ref, self.rows, self.face * self.members + member, 1)

    def own(self):
        return pltpu.make_async_copy(self.src, self.at(self.member), self.sems.at[0, 0])

    def send(self, j):
        to = (self.member + j) % self.members
        return rcopy(
            self.src, self.at(self.member), self.sems.at[0, j], self.sems.at[1, j], member=to
        )

    def came(self, j):
        origin = (self.member + self.members - j) % self.members
        return rcopy(
            self.src, self.at(origin), self.sems.at[0, j], self.sems.at[1, j], member=origin
        )

    def start(self):
        self.own().start()
        for j in range(1, self.members):
            self.send(j).start()

    def wait(self):
        self.own().wait()
        for j in range(1, self.members):
            self.came(j).wait_recv()
            self.send(j).wait_send()


def coded(v):
    axes = tuple(range(v.ndim - 1))
    most = jnp.max(jnp.abs(v), axis=axes, keepdims=True)
    code = jnp.round(v * (TOP / jnp.maximum(most, 1e-33))).astype(jnp.int32).astype(i16)
    most = most.reshape(1, v.shape[-1])
    return code, jnp.broadcast_to(most * (1.0 / TOP), (8, v.shape[-1]))


def decoded(code, scale):
    return code.astype(jnp.int32).astype(f32) * scale[0:1, :]


class Scatter:
    def __init__(self, g, chips, members, scratch, sems):
        self.g, self.chips, self.members = g, chips, members
        self.fromcore, self.acc, self.out1, self.in1, self.out2, self.in2 = scratch[:6]
        self.sc = scratch[6:]
        self.sems = sems
        face = lax.axis_index("face")
        self.member = lax.axis_index("member")
        self.core, self.chip = face % 2, face // 2
        self.partner = self.chip * 2 + 1 - self.core
        self.order = list(range(1, chips)) + [0]

    def part(self, chip, core):
        return pl.ds((chip * 2 + core) * self.members, self.members)

    def there(self, j):
        return (self.chip + j) % self.chips

    def core_copy(self, j):
        return rcopy(
            self.g.at[self.part(self.there(j), 1 - self.core)],
            self.fromcore.at[j],
            self.sems.at[0, j],
            self.sems.at[1, j],
            face=self.partner,
        )

    def copies(self, first, boxes, j, **to):
        s = self.sems
        return [
            rcopy(a.at[j], b.at[j], s.at[i, j], s.at[i + 1, j], **to)
            for i, (a, b) in zip((first, first + 2), boxes)
        ]

    def chip_copies(self, j):
        boxes = [(self.out1, self.in1)] + ([(self.sc[0], self.sc[1])] if self.sc else [])
        return self.copies(2, boxes, j, face=self.there(j) * 2 + self.core)

    def line_copies(self, j):
        boxes = [(self.out2, self.in2)] + ([(self.sc[2], self.sc[3])] if self.sc else [])
        return self.copies(6, boxes, j, member=(self.member + j) % self.members)

    def core_start(self):
        for j in self.order:
            self.core_copy(j).start()

    def core_done(self):
        for j in self.order:
            self.core_copy(j).wait_recv()
            total = self.g[self.part(self.there(j), self.core)] + self.fromcore[j]
            if j == 0:
                self.acc[...] = total
                continue
            if self.sc:
                self.out1[j], self.sc[0][j] = coded(total)
            else:
                self.out1[j] = total
            for c in self.chip_copies(j):
                c.start()

    def summed(self, to):
        v = self.acc[to]
        for i in range(1, self.chips):
            piece = self.in1[i, to]
            v = v + (decoded(piece, self.sc[1][i]) if self.sc else piece)
        return v

    def chip_done(self):
        for j in range(1, self.chips):
            for c in self.chip_copies(j):
                c.wait_recv()
        for j in range(1, self.members):
            v = self.summed((self.member + j) % self.members)
            if self.sc:
                self.out2[j], self.sc[2][j] = coded(v)
            else:
                self.out2[j] = v
            for c in self.line_copies(j):
                c.start()

    def line_done(self):
        total = self.summed(self.member)
        for j in range(1, self.members):
            for c in self.line_copies(j):
                c.wait_recv()
            piece = self.in2[j]
            total = total + (decoded(piece, self.sc[3][j]) if self.sc else piece)
        return total

    def finish(self):
        for j in range(self.chips):
            self.core_copy(j).wait_send()
        for j in range(1, self.chips):
            for c in self.chip_copies(j):
                c.wait_send()
        for j in range(1, self.members):
            for c in self.line_copies(j):
                c.wait_send()


def scatter_scratch(chips, members, rows, lanes, code):
    kind = i16 if code else f32
    out = [
        VMEM((chips, members, rows, lanes), f32),
        VMEM((members, rows, lanes), f32),
        VMEM((chips, members, rows, lanes), kind),
        VMEM((chips, members, rows, lanes), kind),
        VMEM((members, rows, lanes), kind),
        VMEM((members, rows, lanes), kind),
    ]
    if code:
        out += [VMEM((chips, 8, lanes), f32)] * 2 + [VMEM((members, 8, lanes), f32)] * 2
    return out


def put_rows(ref, first, v):
    rows, done = ref.shape[1], 0
    while done < v.shape[0]:
        block, at = divmod(first + done, rows)
        size = min(rows - at, v.shape[0] - done)
        ref[block, at : at + size, :] = v[done : done + size]
        done += size


def sides_of(field):
    h, w, c = field.shape
    return [
        field[0],
        field[:, w - 1 : w, :].reshape(h, c),
        field[h - 1],
        field[:, 0:1, :].reshape(h, c),
    ]


def g_of(v):
    return v * lax.rsqrt(v * v + smooth_sq)


class Step:
    def __init__(self, dims, refs):
        self.__dict__.update(dims)
        self.__dict__.update(refs)
        face = lax.axis_index("face")
        self.face, self.member = face, lax.axis_index("member")


    def tables(self):
        first = self.face * self.T
        total = self.place.shape[0]

        def fill(i, carry):
            tile = self.place[first + i]
            for a in range(4):
                base = (tile * 4 + a) * 3
                want = self.glue[base]

                def look(s, slot):
                    return jnp.where(self.place[s] == want, s, slot)

                slot = lax.fori_loop(0, total, look, jnp.int32(0), unroll=8)
                owner = slot // self.T
                self.at_face[i * 4 + a] = owner
                self.at_slot[i * 4 + a] = slot - owner * self.T
                self.at_side[i * 4 + a] = self.glue[base + 1]
            size = 4 * self.w
            row = lax.broadcasted_iota(jnp.int32, (size, size), 0)
            col = lax.broadcasted_iota(jnp.int32, (size, size), 1)
            side = row // self.w
            at = row - side * self.w
            flag = jnp.zeros((size, size), jnp.int32)
            for a in range(4):
                flag = jnp.where(side == a, self.glue[(tile * 4 + a) * 3 + 2], flag)
            target = side * self.w + jnp.where(flag == 1, self.w - 1 - at, at)
            self.turn[i] = jnp.where(col == target, 1.0, 0.0).astype(bf16)
            return carry

        lax.fori_loop(0, self.T, fill, 0)

    def rims_from(self, box, m):
        def one(i, carry):
            cat = jnp.concatenate(
                [
                    box[self.at_face[i * 4 + a], self.at_slot[i * 4 + a] * 4 + self.at_side[i * 4 + a]]
                    for a in range(4)
                ],
                axis=0,
            )
            self.rims[m * self.T + i] = mm(self.turn[i], cat)
            return carry

        lax.fori_loop(0, self.T, one, 0)

    def cut(self, box, i):
        for a, v in enumerate(sides_of(self.field)):
            box[self.face, i * 4 + a] = v.astype(bf16)

    def cut_input(self, m):
        def one(i, carry):
            v = self.x[m * self.T + i].astype(f32)
            self.field[...] = v.reshape(self.h, self.w, self.c)
            self.cut(self.edges_x[m], i)
            return carry

        lax.fori_loop(0, self.T, one, 0)


    def conv(self, u, src, x3, w_ref, slope):
        h, w, c, G = self.h, self.w, self.c, self.G
        k0 = u * G
        pad = self.pad
        for g in range(G):
            k = k0 + g
            rims = self.rims[k]
            pad[1 : h + 1, 8 : 8 + w, :] = src[k].reshape(h, w, c).astype(f32)
            pad[0, 8 : 8 + w, :] = rims[0:w]
            pad[1 : h + 1, 8 + w : 9 + w, :] = rims[w : w + h].reshape(h, 1, c)
            pad[h + 1, 8 : 8 + w, :] = rims[w + h : 2 * w + h]
            pad[1 : h + 1, 7:8, :] = rims[2 * w + h :].reshape(h, 1, c)
            for b in range(3):
                x3[k, :, :, b * c : (b + 1) * c] = pad[:, 7 + b : 7 + b + w, :].astype(bf16)
        pre = None
        for a in range(3):
            part = mm(
                x3[pl.ds(k0, G), a : a + h].reshape(G * h * w, 3 * c),
                w_ref[3 * a * c : 3 * (a + 1) * c, :],
            )
            pre = part if pre is None else pre + part
        s = 1.0 / (1.0 + jnp.exp(-pre))
        act = pre * s
        slope[pl.ds(k0, G)] = (s + act * (1.0 - s)).reshape(G, h * w, c)
        return act.astype(bf16)

    def conv_first(self, u):
        act = self.conv(u, self.x, self.x3_one, self.w1, self.d_one)
        cells = self.h * self.w
        for g in range(self.G):
            self.act_one[u * self.G + g] = act[g * cells : (g + 1) * cells]

    def cut_act(self, m):
        h, w, c = self.h, self.w, self.c

        def one(i, carry):
            self.field[...] = self.act_one[m * self.T + i].astype(f32).reshape(h, w, c)
            self.cut(self.edges_a[m], i)
            return carry

        lax.fori_loop(0, self.T, one, 0)

    def go(self, u, j):
        to = (self.member + j) % self.Z
        return rcopy(
            self.packed.at[u, to],
            self.came.at[u, j],
            self.ssem.at[0, u, j],
            self.ssem.at[1, u, j],
            member=to,
        )

    def home(self, i, j, here=False):
        back = (self.member + j) % self.Z if here else self.member
        return rcopy(
            self.slopes.at[i, j],
            self.back.at[i, back],
            self.ssem.at[2, i, j],
            self.ssem.at[3, i, j],
            member=(self.member + self.Z - j) % self.Z,
        )

    def conv_last(self, u):
        act = self.conv(u, self.act_one, self.x3_two, self.w2, self.d_two)
        G, cells, part = self.G, self.h * self.w, self.part
        outs = []
        for g in range(G):
            own = act[g * cells : (g + 1) * cells]
            self.act_two[u * G + g] = own
            outs.append(mm(self.head_t[0 : self.V, :], own, NT).astype(bf16))
        for q in range(self.Z):
            cols = [o[:, q * part : (q + 1) * part] for o in outs]
            self.packed[u, q] = jnp.concatenate(cols, axis=1) if G > 1 else cols[0]
        for j in range(1, self.Z):
            self.go(u, j).start()


    def score(self, p):
        ensemble = self.H * self.Z
        for m in range(self.H):
            for j in range(1, self.Z):
                self.go(m * self.P + p, j).wait_recv()
        rows = 16 if self.V % 16 == 0 else self.V
        for r in range(0, self.V, rows):
            at = slice(r, r + rows)
            o = [self.obs[p * self.G + g, at, :].astype(f32) for g in range(self.G)]
            o = jnp.concatenate(o, axis=1) if self.G > 1 else o[0]
            names = [(m, j) for j in range(self.Z) for m in range(self.H)]
            vals = []
            for m, j in names:
                u = m * self.P + p
                v = self.packed[u, self.member, at, :] if j == 0 else self.came[u, j, at, :]
                vals.append(v.astype(f32))
            paired = [None] * len(vals)
            for a in range(len(vals)):
                for b in range(a + 1, len(vals)):
                    t = g_of(vals[a] - vals[b])
                    paired[a] = t if paired[a] is None else paired[a] + t
                    paired[b] = -t if paired[b] is None else paired[b] - t
            for (m, j), v, t in zip(names, vals, paired):
                i = p * self.H + m
                s = (g_of(v - o) / ensemble - t / (ensemble * ensemble)) / self.h
                if j == 0:
                    self.back[i, self.member, at, :] = s.astype(bf16)
                else:
                    self.slopes[i, j, at, :] = s.astype(bf16)
        for m in range(self.H):
            for j in range(1, self.Z):
                self.home(p * self.H + m, j).start()


    def prepare_back(self):
        c = self.c
        for a in range(3):
            for b in range(3):
                tap = self.w2[(3 * a + b) * c : (3 * a + b + 1) * c, :]
                self.va[a, :, b * c : (b + 1) * c] = tap
                if b == 0:
                    self.vb[0, :, a * c : (a + 1) * c] = tap
                if b == 2:
                    self.vb[1, :, a * c : (a + 1) * c] = tap
        self.hg[...] = jnp.zeros_like(self.hg)
        self.pad2[...] = jnp.zeros_like(self.pad2)

    def lanes(self, k):
        cells = self.h * self.w
        return pl.ds(pl.multiple_of(k * cells, cells), cells)

    def backward(self, i):
        h, w, c, G, H, part = self.h, self.w, self.c, self.G, self.H, self.part
        p = i // H
        m = i - p * H
        u = m * self.P + p
        for j in range(1, self.Z):
            self.home(i, j, here=True).wait_recv()
        pad = self.pad2
        for g in range(G):
            k = u * G + g
            slope_out = jnp.concatenate(
                [self.back[i, q][:, g * part : (g + 1) * part] for q in range(self.Z)], axis=1
            )
            self.hg[0 : self.V, :] += mm(slope_out, self.act_two[k])
            back = mm(slope_out, self.head_t[0 : self.V, :], TN)
            slope = (back * self.d_two[k]).astype(bf16)
            self.turned[:, self.lanes(k)] = slope.T
            pad[2 : h + 2, 8 : 8 + w, :] = slope.astype(f32).reshape(h, w, c)
            for b in range(3):
                self.s3[g, :, :, b * c : (b + 1) * c] = pad[:, 9 - b : 9 - b + w, :].astype(bf16)
            left = pad[:, 8:9, :].reshape(h + 4, c)
            right = pad[:, 7 + w : 8 + w, :].reshape(h + 4, c)
            for a in range(3):
                self.cols[0, g, :, a * c : (a + 1) * c] = left[3 - a : 3 - a + h].astype(bf16)
                self.cols[1, g, :, a * c : (a + 1) * c] = right[3 - a : 3 - a + h].astype(bf16)
        full = None
        for a in range(3):
            lhs = self.s3[:, 2 - a : 4 - a + h].reshape(G * (h + 2) * w, 3 * c)
            one = mm(lhs, self.va[a], NT)
            full = one if full is None else full + one
        full = full.reshape(G, h + 2, w, c).astype(bf16)
        self.inner[pl.ds(u * G, G)] = full[:, 1 : h + 1]
        lefts = mm(self.cols[0].reshape(G * h, 3 * c), self.vb[0], NT).astype(bf16)
        rights = mm(self.cols[1].reshape(G * h, 3 * c), self.vb[1], NT).astype(bf16)
        for g in range(G):
            at = (i * G + g) * 4
            sides = (
                full[g, 0],
                rights[g * h : (g + 1) * h],
                full[g, h + 1],
                lefts[g * h : (g + 1) * h],
            )
            for a in range(4):
                self.borders[self.face, at + a] = sides[a]

    def rims_back(self, m):
        G = self.G

        def one(i, carry):
            sides = []
            for a in range(4):
                at = i * 4 + a
                slot = self.at_slot[at]
                unit = slot // G
                j = (m * G + slot - unit * G) * 4 + self.at_side[at]
                sides.append(self.borders[self.at_face[at], unit * (self.H * G * 4) + j])
            self.rims[m * self.T + i] = mm(self.turn[i], jnp.concatenate(sides, axis=0))
            return carry

        lax.fori_loop(0, self.T, one, 0)

    def slope_first(self, k):
        h, w, c = self.h, self.w, self.c
        rims, field = self.rims[k], self.field
        field[...] = self.inner[k].astype(f32)
        field[0] += rims[0:w]
        field[:, w - 1 : w, :] += rims[w : w + h].reshape(h, 1, c)
        field[h - 1] += rims[w + h : 2 * w + h]
        field[:, 0:1, :] += rims[2 * w + h :].reshape(h, 1, c)
        slope = (field[...].reshape(h * w, c) * self.d_one[k]).astype(bf16)
        self.turned[:, self.lanes(k)] = slope.T

    def products(self, kb, x3):
        h, w, c, K = self.h, self.w, self.c, self.K
        cells = h * w
        at = pl.ds(pl.multiple_of(kb * K * cells, K * cells), K * cells)
        for a in range(3):
            rhs = x3[pl.ds(kb * K, K), a : a + h].reshape(K * cells, 3 * c)
            self.acc[a] += mm(self.turned[:, at], rhs)

    def turn_out(self, ref):
        c = self.c
        for a in range(3):
            for b in range(3):
                put_rows(ref, (3 * a + b) * c, self.acc[a, :, b * c : (b + 1) * c].T)
        self.acc[...] = jnp.zeros_like(self.acc)


def hooked(steps, body, before=None, after=None):
    before, after = before or {}, after or {}

    def one(i, carry):
        for s, todo in sorted(before.items()):
            pl.when(i == s)(todo)
        body(i)
        for s, todo in sorted(after.items()):
            pl.when(i == s)(todo)
        return carry

    lax.fori_loop(0, steps, one, 0)


def merge(*items):
    out = {}
    for at, todo in items:
        out.setdefault(at, []).append(todo)

    def run(todos):
        def go():
            for t in todos:
                t()

        return go

    return {at: run(todos) for at, todos in out.items()}


def step_kernel(dims, names, *refs):
    s = Step(dims, dict(zip(names, refs)))
    chips, members, H, PU = s.chips, s.Z, s.H, s.P
    gsem = s.gsem
    s.edges_x = [getattr(s, f"edges_x{m}") for m in range(H)]
    s.edges_a = [getattr(s, f"edges_a{m}") for m in range(H)]
    w1, w2, heads = [
        getattr(s, name + "_apart") if hasattr(s, name + "_apart") else getattr(s, name)
        for name in ("w1", "w2", "heads")
    ]

    def settle(name, rows):
        if hasattr(s, name + "_apart"):
            apart, whole = getattr(s, name + "_apart"), getattr(s, name)
            for d in range(apart.shape[0]):
                whole[d * rows : (d + 1) * rows, :] = apart[d]

    lw1 = LineGather(s.weights.at[0], w1, s.rows, members, s.lsem.at[0])
    lw2 = LineGather(s.weights.at[1], w2, s.rows, members, s.lsem.at[1])
    lhd = LineGather(s.head_own, heads, s.hrows, members, s.lsem.at[2])
    gw1 = gather_rows(w1, s.rows, members, chips, gsem.at[0])
    gw2 = gather_rows(w2, s.rows, members, chips, gsem.at[1])
    ghd = gather_rows(heads, s.hrows, members, chips, gsem.at[2])
    sides, share = s.T * 4, H * s.G * 4
    gx = [gather_edges(s.edges_x[m], 0, sides, chips, gsem.at[3 + m]) for m in range(H)]
    ga = [gather_edges(s.edges_a[m], 0, sides, chips, gsem.at[3 + H + m]) for m in range(H)]
    gb = [
        gather_edges(s.borders, p * share, share, chips, gsem.at[3 + 2 * H + p])
        for p in range(PU)
    ]

    s.head_own[...] = jnp.zeros_like(s.head_own)
    s.head_own[:, 0 : s.V] = s.head[...]
    s.cut_input(0)
    greet(chips, members)
    lw1.start()
    gx[0].start()
    lw2.start()
    lhd.start()
    for m in range(1, H):
        s.cut_input(m)
    s.tables()
    s.pad[...] = jnp.zeros_like(s.pad)
    lw1.wait()
    gw1.start()
    gx[0].relay_first()
    lw2.wait()
    lhd.wait()
    gx[0].relay_rest()
    gw1.relay_first()
    gw1.relay_rest()
    for m in range(1, H):
        gx[m].start()
    gw2.start()
    ghd.start()
    gw1.finish()
    settle("w1", s.rows)

    last = H * PU - 1

    def ready_x(m):
        gx[m].finish()
        s.rims_from(s.edges_x[m], m)

    def send_a(m):
        s.cut_act(m)
        ga[m].start()

    def ready_a(m):
        ga[m].finish()
        s.rims_from(s.edges_a[m], m)

    before = {m * PU: functools.partial(ready_x, m) for m in range(H)}
    after = []
    for m in range(1, H):
        after.append((max(m * PU - 3, 0), gx[m].relay_first))
        after.append((m * PU - 2 if PU > 1 else 0, gx[m].relay_rest))
    for m in range(H - 1):
        after.append(((m + 1) * PU - 1, functools.partial(send_a, m)))
    after.append((min(PU, last), gw2.relay_first))
    after.append((min(PU, last), ghd.relay_first))
    after.append((min(PU + 1, last), gw2.relay_rest))
    after.append((min(PU + 1, last), ghd.relay_rest))
    for m in range(H - 1):
        after.append((min((m + 1) * PU + 2, last), ga[m].relay_first))
    hooked(H * PU, s.conv_first, before, merge(*after))
    s.cut_act(H - 1)
    for m in range(H - 1):
        ga[m].relay_rest()
    ga[H - 1].start()
    gw2.finish()
    ghd.finish()
    settle("w2", s.rows)
    settle("heads", s.hrows)
    s.head_t[...] = s.heads[...].astype(f32).T.astype(bf16)

    before = {m * PU: functools.partial(ready_a, m) for m in range(H)}
    after = [
        (max((H - 1) * PU - 2, 0), ga[H - 1].relay_first),
        (max((H - 1) * PU - 1, 0), ga[H - 1].relay_rest),
    ]
    hooked(H * PU, s.conv_last, before, merge(*after))
    s.prepare_back()

    lax.fori_loop(0, PU, lambda p, carry: (s.score(p), carry)[1], 0)
    after = []
    late = []
    total = H * PU
    for p in range(PU):
        at = (p + 1) * H - 1
        after.append((at, gb[p].start))
        for step, todo in ((at + 2, gb[p].relay_first), (at + 4, gb[p].relay_rest)):
            if step < total:
                after.append((step, todo))
            else:
                late.append((min(step - total, s.n // s.K - 1), todo))
    hooked(total, s.backward, None, merge(*after))

    s.acc[...] = jnp.zeros_like(s.acc)
    hooked(s.n // s.K, lambda kb: s.products(kb, s.x3_two), None, merge(*late))
    s_two = Scatter(s.two, chips, members, [getattr(s, f"t{i}") for i in range(10)], s.csem.at[0])
    s_head = Scatter(s.hg_t, chips, members, [getattr(s, f"h{i}") for i in range(6)], s.csem.at[1])
    s_one = Scatter(s.one, chips, members, [getattr(s, f"o{i}") for i in range(10)], s.csem.at[2])
    s.turn_out(s.two)
    put_rows(s.hg_t, 0, s.hg[...].T)
    s_two.core_start()
    s_head.core_start()

    for p in range(PU):
        gb[p].finish()
    for m in range(H):
        s.rims_back(m)
    lax.fori_loop(0, s.n, lambda k, carry: (s.slope_first(k), carry)[1], 0)
    s_two.core_done()
    s_head.core_done()

    def pass_on():
        s_two.chip_done()
        s_head.chip_done()

    mid = max(s.n // s.K - 2, 0)
    hooked(s.n // s.K, lambda kb: s.products(kb, s.x3_one), None, {mid: pass_on})
    s.turn_out(s.one)
    s_one.core_start()
    s_one.core_done()
    s.two_out[...] = s_two.line_done()
    s.head_out[...] = s_head.line_done()[:, 0 : s.V]
    s_one.chip_done()
    s.one_out[...] = s_one.line_done()
    for scatter in (s_two, s_head, s_one):
        scatter.finish()
    for u in range(H * PU):
        for j in range(1, members):
            s.go(u, j).wait_send()
            s.home(u, j).wait_send()


def shards(faces, zs, features, observed, conv_weights, head_weight, adjacency, placement_map):
    H, T, h, w, c = features.shape
    n = H * T
    V = head_weight.shape[1]
    rows, hrows = conv_weights.shape[0], head_weight.shape[0]
    lanes = -(-V // 128) * 128
    chips = faces // 2
    G = 2 if T % 2 == 0 else 1
    PU = T // G
    K = 4 if n % 4 == 0 else (2 if n % 2 == 0 else 1)
    part = observed.shape[-1]
    cells = h * w
    dims = dict(
        H=H, T=T, h=h, w=w, c=c, n=n, V=V, rows=rows, hrows=hrows, chips=chips, Z=zs, G=G, P=PU,
        K=K, part=part,
    )
    side = 4 * w
    total_rows = rows * faces * zs
    total_heads = hrows * faces * zs
    scratch = {
        "at_face": SMEM((T * 4,), jnp.int32),
        "at_slot": SMEM((T * 4,), jnp.int32),
        "at_side": SMEM((T * 4,), jnp.int32),
        "turn": VMEM((T, side, side), bf16),
        "rims": VMEM((n, side, c), f32),
        "field": VMEM((h, w, c), f32),
        "pad": VMEM((h + 2, w + 16, c), f32),
        "pad2": VMEM((h + 4, w + 16, c), f32),
        "head_own": VMEM((hrows, lanes), bf16),
        "w1": VMEM((total_rows, c), bf16),
        "w2": VMEM((total_rows, c), bf16),
        "heads": VMEM((total_heads, lanes), bf16),
        "head_t": VMEM((lanes, total_heads), bf16),
        "x3_one": VMEM((n, h + 2, w, 3 * c), bf16),
        "x3_two": VMEM((n, h + 2, w, 3 * c), bf16),
        "d_one": VMEM((n, cells, c), f32),
        "d_two": VMEM((n, cells, c), f32),
        "act_one": VMEM((n, cells, c), bf16),
        "act_two": VMEM((n, cells, c), bf16),
        "packed": VMEM((H * PU, zs, V, G * part), bf16),
        "came": VMEM((H * PU, zs, V, G * part), bf16),
        "slopes": VMEM((H * PU, zs, V, G * part), bf16),
        "back": VMEM((H * PU, zs, V, G * part), bf16),
        "va": VMEM((3, c, 3 * c), bf16),
        "vb": VMEM((2, c, 3 * c), bf16),
        "s3": VMEM((G, h + 4, w, 3 * c), bf16),
        "cols": VMEM((2, G, h, 3 * c), bf16),
        "inner": VMEM((n, h, w, c), bf16),
        "turned": VMEM((c, n * cells), bf16),
        "acc": VMEM((3, c, 3 * c), f32),
        "hg": VMEM((lanes, c), f32),
        "hg_t": VMEM((faces * zs, hrows, lanes), f32),
        "one": VMEM((faces * zs, rows, c), f32),
        "two": VMEM((faces * zs, rows, c), f32),
        "borders": VMEM((faces, PU * H * G * 4, w, c), bf16),
    }
    for m in range(H):
        scratch[f"edges_x{m}"] = VMEM((faces, T * 4, w, c), bf16)
        scratch[f"edges_a{m}"] = VMEM((faces, T * 4, w, c), bf16)
    for name, r, lane, code in (("t", rows, c, True), ("h", hrows, lanes, False), ("o", rows, c, True)):
        for i, v in enumerate(scatter_scratch(chips, zs, r, lane, code)):
            scratch[f"{name}{i}"] = v
    if rows % 16:
        for name in ("w1_apart", "w2_apart"):
            scratch[name] = VMEM((faces * zs, rows, c), bf16)
    if hrows % 16:
        scratch["heads_apart"] = VMEM((faces * zs, hrows, lanes), bf16)
    dma = pltpu.SemaphoreType.DMA
    scratch["gsem"] = dma((3 + 2 * H + PU, 4, chips + 3))
    scratch["lsem"] = dma((3, 2, zs))
    scratch["ssem"] = dma((4, H * PU, zs))
    scratch["csem"] = dma((3, 10, max(chips, zs)))
    vmem = pl.BlockSpec(memory_space=VMEM)
    smem = pl.BlockSpec(memory_space=SMEM)
    ins = ["place", "glue", "x", "obs", "weights", "head"]
    outs = ["one_out", "two_out", "head_out"]
    one, two, head_out = pl.pallas_call(
        functools.partial(step_kernel, dims, ins + outs + list(scratch)),
        out_shape=[
            jax.ShapeDtypeStruct((rows, c), f32),
            jax.ShapeDtypeStruct((rows, c), f32),
            jax.ShapeDtypeStruct((hrows, V), f32),
        ],
        in_specs=[smem, smem] + [vmem] * 4,
        out_specs=[vmem] * 3,
        scratch_shapes=list(scratch.values()),
        compiler_params=pltpu.CompilerParams(
            collective_id=1, has_side_effects=True, vmem_limit_bytes=LIMIT
        ),
        name="step",
    )(
        placement_map,
        adjacency.reshape(-1),
        features.reshape(n, cells, c),
        observed,
        conv_weights.transpose(1, 0, 2),
        head_weight,
    )
    return jnp.stack([one, two], axis=1), head_out


def solution(mesh):
    in_specs = (
        P("member", "face", None, None, None),
        P("face", None, "member"),
        P(("face", "member"), None, None),
        P(("face", "member"), None),
        P(),
        P(),
    )
    out_specs = (P(("face", "member"), None, None), P(("face", "member"), None))
    body = functools.partial(shards, mesh.shape["face"], mesh.shape["member"])
    return jax.shard_map(body, mesh=mesh, in_specs=in_specs, out_specs=out_specs, check_vma=False)
```

```python
import functools

import jax
import jax.numpy as jnp
from jax import lax
from jax.experimental import pallas as pl
from jax.experimental.pallas import tpu as pltpu
from jax.sharding import PartitionSpec as P

smooth_sq = 0.0625
MESH = pl.DeviceIdType.MESH
VMEM = pltpu.VMEM
SMEM = pltpu.SMEM
f32 = jnp.float32
bf16 = jnp.bfloat16
i16 = jnp.int16
LIMIT = 62 * 1024 * 1024
TOP = 32767.0
NT = (((1,), (1,)), ((), ()))
TN = (((0,), (0,)), ((), ()))
NN = (((1,), (0,)), ((), ()))


def mm(a, b, dims=NN):
    return lax.dot_general(a, b, dims, preferred_element_type=f32)


def rcopy(src, dst, send, recv, **where):
    return pltpu.make_async_remote_copy(
        src_ref=src, dst_ref=dst, send_sem=send, recv_sem=recv, device_id=where, device_id_type=MESH
    )


def greet(chips, members):
    face = lax.axis_index("face")
    member = lax.axis_index("member")
    core = face % 2
    chip = face // 2
    barrier = pltpu.get_barrier_semaphore()
    pl.semaphore_signal(
        barrier, inc=1, device_id={"face": chip * 2 + 1 - core}, device_id_type=MESH
    )
    for j in range(1, chips):
        pl.semaphore_signal(
            barrier,
            inc=1,
            device_id={"face": ((chip + j) % chips) * 2 + core},
            device_id_type=MESH,
        )
    for j in range(1, members):
        pl.semaphore_signal(
            barrier, inc=1, device_id={"member": (member + j) % members}, device_id_type=MESH
        )
    pl.semaphore_wait(barrier, chips + members - 1)


class FaceGather:
    def __init__(self, at, chips, sems):
        self.at, self.chips, self.sems = at, chips, sems
        face = lax.axis_index("face")
        self.face, self.core, self.chip = face, face % 2, face // 2
        self.partner = self.chip * 2 + 1 - self.core

    def direct(self, j):
        mine = self.at(self.face, None)
        return rcopy(
            mine,
            mine,
            self.sems.at[0, j],
            self.sems.at[1, j],
            face=((self.chip + j) % self.chips) * 2 + self.core,
        )

    def forward(self, j):
        block = self.at(((self.chip + self.chips - j) % self.chips) * 2 + self.core, None)
        return rcopy(block, block, self.sems.at[2, j], self.sems.at[3, j], face=self.partner)

    def start(self):
        for j in range(1, self.chips):
            self.direct(j).start()
        self.forward(0).start()

    def relay_first(self):
        pass

    def relay_rest(self):
        for j in range(1, self.chips):
            self.direct(j).wait_recv()
            self.forward(j).start()

    def finish(self):
        for j in range(1, self.chips):
            self.direct(j).wait_send()
        for j in range(self.chips):
            self.forward(j).wait()


class SquareGather:
    def __init__(self, at, chips, sems):
        self.at, self.sems = at, sems
        face = lax.axis_index("face")
        core, chip = face % 2, face // 2
        col, row = chip % 2, chip // 2
        self.face = face
        self.partner = chip * 2 + 1 - core
        self.beside = (row * 2 + 1 - col) * 2 + core
        self.below = ((1 - row) * 2 + col) * 2 + core
        self.across = ((1 - row) * 2 + 1 - col) * 2 + core

    def direct(self, k):
        to = (self.beside, self.beside, self.below, self.below, self.below, self.beside)[k]
        block = (self.face,) * 4 + (self.beside, self.below)
        ref = self.at(block[k], (0, 1, 1, 0, 0, 1)[k])
        return rcopy(ref, ref, self.sems.at[0, k], self.sems.at[1, k], face=to)

    def forward(self, k):
        if k == 6:
            ref = self.at(self.face, None)
        else:
            block = (
                self.beside,
                self.beside,
                self.below,
                self.below,
                self.across,
                self.across,
            )
            ref = self.at(block[k], (0, 1, 1, 0, 0, 1)[k])
        return rcopy(ref, ref, self.sems.at[2, k], self.sems.at[3, k], face=self.partner)

    def start(self):
        for k in (0, 2, 1, 3):
            self.direct(k).start()
        self.forward(6).start()

    def relay_first(self):
        for k, onward in ((0, 4), (2, 5)):
            self.direct(k).wait_recv()
            self.direct(onward).start()
            self.forward(k).start()

    def relay_rest(self):
        for k in (1, 3, 4, 5):
            self.direct(k).wait_recv()
            self.forward(k).start()

    def finish(self):
        for k in range(6):
            self.direct(k).wait_send()
        for k in range(7):
            self.forward(k).wait()


def units(ref, rows, start, count):
    if len(ref.shape) == 3:
        return ref.at[pl.ds(start, count)] if count > 1 else ref.at[start]
    return ref.at[pl.ds(pl.multiple_of(start * rows, rows), count * rows)]


def gather_rows(ref, rows, members, chips, sems):
    def at(block, part):
        if part is None:
            return units(ref, rows, block * members, members)
        half = members // 2
        return units(ref, rows, block * members + part * half, half)

    return (SquareGather if chips == 4 and members % 2 == 0 else FaceGather)(at, chips, sems)


def gather_edges(ref, start, count, chips, sems):
    def at(block, part):
        if part is None:
            return ref.at[block, pl.ds(start, count)]
        half = count // 2
        return ref.at[block, pl.ds(start + part * half, half)]

    return (SquareGather if chips == 4 and count % 2 == 0 else FaceGather)(at, chips, sems)


class LineGather:
    def __init__(self, src, ref, rows, members, sems):
        self.src, self.ref, self.rows, self.members, self.sems = src, ref, rows, members, sems
        self.face, self.member = lax.axis_index("face"), lax.axis_index("member")

    def at(self, member):
        return units(self.ref, self.rows, self.face * self.members + member, 1)

    def own(self):
        return pltpu.make_async_copy(self.src, self.at(self.member), self.sems.at[0, 0])

    def send(self, j):
        to = (self.member + j) % self.members
        return rcopy(
            self.src, self.at(self.member), self.sems.at[0, j], self.sems.at[1, j], member=to
        )

    def came(self, j):
        origin = (self.member + self.members - j) % self.members
        return rcopy(
            self.src, self.at(origin), self.sems.at[0, j], self.sems.at[1, j], member=origin
        )

    def start(self):
        self.own().start()
        for j in range(1, self.members):
            self.send(j).start()

    def wait(self):
        self.own().wait()
        for j in range(1, self.members):
            self.came(j).wait_recv()
            self.send(j).wait_send()


def coded(v):
    axes = tuple(range(v.ndim - 1))
    most = jnp.max(jnp.abs(v), axis=axes, keepdims=True)
    code = jnp.round(v * (TOP / jnp.maximum(most, 1e-33))).astype(jnp.int32).astype(i16)
    most = most.reshape(1, v.shape[-1])
    return code, jnp.broadcast_to(most * (1.0 / TOP), (8, v.shape[-1]))


def decoded(code, scale):
    return code.astype(jnp.int32).astype(f32) * scale[0:1, :]


class Scatter:
    def __init__(self, g, chips, members, scratch, sems):
        self.g, self.chips, self.members = g, chips, members
        self.fromcore, self.acc, self.out1, self.in1, self.out2, self.in2 = scratch[:6]
        self.sc = scratch[6:]
        self.sems = sems
        face = lax.axis_index("face")
        self.member = lax.axis_index("member")
        self.core, self.chip = face % 2, face // 2
        self.partner = self.chip * 2 + 1 - self.core
        self.order = list(range(1, chips)) + [0]

    def part(self, chip, core):
        return pl.ds((chip * 2 + core) * self.members, self.members)

    def there(self, j):
        return (self.chip + j) % self.chips

    def core_copy(self, j):
        return rcopy(
            self.g.at[self.part(self.there(j), 1 - self.core)],
            self.fromcore.at[j],
            self.sems.at[0, j],
            self.sems.at[1, j],
            face=self.partner,
        )

    def copies(self, first, boxes, j, **to):
        s = self.sems
        return [
            rcopy(a.at[j], b.at[j], s.at[i, j], s.at[i + 1, j], **to)
            for i, (a, b) in zip((first, first + 2), boxes)
        ]

    def chip_copies(self, j):
        boxes = [(self.out1, self.in1)] + ([(self.sc[0], self.sc[1])] if self.sc else [])
        return self.copies(2, boxes, j, face=self.there(j) * 2 + self.core)

    def line_copies(self, j):
        boxes = [(self.out2, self.in2)] + ([(self.sc[2], self.sc[3])] if self.sc else [])
        return self.copies(6, boxes, j, member=(self.member + j) % self.members)

    def core_start(self):
        for j in self.order:
            self.core_copy(j).start()

    def core_done(self):
        for j in self.order:
            self.core_copy(j).wait_recv()
            total = self.g[self.part(self.there(j), self.core)] + self.fromcore[j]
            if j == 0:
                self.acc[...] = total
                continue
            if self.sc:
                self.out1[j], self.sc[0][j] = coded(total)
            else:
                self.out1[j] = total
            for c in self.chip_copies(j):
                c.start()

    def summed(self, to):
        v = self.acc[to]
        for i in range(1, self.chips):
            piece = self.in1[i, to]
            v = v + (decoded(piece, self.sc[1][i]) if self.sc else piece)
        return v

    def chip_done(self):
        for j in range(1, self.chips):
            for c in self.chip_copies(j):
                c.wait_recv()
        for j in range(1, self.members):
            v = self.summed((self.member + j) % self.members)
            if self.sc:
                self.out2[j], self.sc[2][j] = coded(v)
            else:
                self.out2[j] = v
            for c in self.line_copies(j):
                c.start()

    def line_done(self):
        total = self.summed(self.member)
        for j in range(1, self.members):
            for c in self.line_copies(j):
                c.wait_recv()
            piece = self.in2[j]
            total = total + (decoded(piece, self.sc[3][j]) if self.sc else piece)
        return total

    def finish(self):
        for j in range(self.chips):
            self.core_copy(j).wait_send()
        for j in range(1, self.chips):
            for c in self.chip_copies(j):
                c.wait_send()
        for j in range(1, self.members):
            for c in self.line_copies(j):
                c.wait_send()


def scatter_scratch(chips, members, rows, lanes, code):
    kind = i16 if code else f32
    out = [
        VMEM((chips, members, rows, lanes), f32),
        VMEM((members, rows, lanes), f32),
        VMEM((chips, members, rows, lanes), kind),
        VMEM((chips, members, rows, lanes), kind),
        VMEM((members, rows, lanes), kind),
        VMEM((members, rows, lanes), kind),
    ]
    if code:
        out += [VMEM((chips, 8, lanes), f32)] * 2 + [VMEM((members, 8, lanes), f32)] * 2
    return out


def put_rows(ref, first, v):
    rows, done = ref.shape[1], 0
    while done < v.shape[0]:
        block, at = divmod(first + done, rows)
        size = min(rows - at, v.shape[0] - done)
        ref[block, at : at + size, :] = v[done : done + size]
        done += size


def sides_of(field):
    h, w, c = field.shape
    return [
        field[0],
        field[:, w - 1 : w, :].reshape(h, c),
        field[h - 1],
        field[:, 0:1, :].reshape(h, c),
    ]


def g_of(v):
    return v * lax.rsqrt(v * v + smooth_sq)


class Step:
    def __init__(self, dims, refs):
        self.__dict__.update(dims)
        self.__dict__.update(refs)
        face = lax.axis_index("face")
        self.face, self.member = face, lax.axis_index("member")


    def tables(self):
        first = self.face * self.T
        total = self.place.shape[0]

        def fill(i, carry):
            tile = self.place[first + i]
            for a in range(4):
                want = self.glue[0, a, tile]

                def look(s, slot):
                    return jnp.where(self.place[s] == want, s, slot)

                slot = lax.fori_loop(0, total, look, jnp.int32(0), unroll=8)
                owner = slot // self.T
                self.at_face[i * 4 + a] = owner
                self.at_slot[i * 4 + a] = slot - owner * self.T
                self.at_side[i * 4 + a] = self.glue[1, a, tile]
            size = 4 * self.w
            row = lax.broadcasted_iota(jnp.int32, (size, size), 0)
            col = lax.broadcasted_iota(jnp.int32, (size, size), 1)
            side = row // self.w
            at = row - side * self.w
            flag = jnp.zeros((size, size), jnp.int32)
            for a in range(4):
                flag = jnp.where(side == a, self.glue[2, a, tile], flag)
            target = side * self.w + jnp.where(flag == 1, self.w - 1 - at, at)
            self.turn[i] = jnp.where(col == target, 1.0, 0.0).astype(bf16)
            return carry

        lax.fori_loop(0, self.T, fill, 0)

    def rims_from(self, box, m):
        def one(i, carry):
            cat = jnp.concatenate(
                [
                    box[self.at_face[i * 4 + a], self.at_slot[i * 4 + a] * 4 + self.at_side[i * 4 + a]]
                    for a in range(4)
                ],
                axis=0,
            )
            self.rims[m * self.T + i] = mm(self.turn[i], cat)
            return carry

        lax.fori_loop(0, self.T, one, 0, unroll=True)

    def turn_inputs(self):
        for p in range(self.P):
            o = [self.obs[p * self.G + g].astype(f32).T for g in range(self.G)]
            self.obs_wide[p] = jnp.concatenate(o, axis=1) if self.G > 1 else o[0]

    def cut(self, box, i):
        for a, v in enumerate(sides_of(self.field)):
            box[self.face, i * 4 + a] = v.astype(bf16)

    def cut_input(self, m):
        def one(i, carry):
            v = self.x[m * self.T + i].astype(f32)
            self.field[...] = v.reshape(self.h, self.w, self.c)
            self.cut(self.edges_x[m], i)
            return carry

        lax.fori_loop(0, self.T, one, 0)


    def conv(self, u, src, x3, w_ref, slope):
        h, w, c, G = self.h, self.w, self.c, self.G
        k0 = u * G
        pad = self.pad
        for g in range(G):
            k = k0 + g
            rims = self.rims[k]
            pad[1 : h + 1, 8 : 8 + w, :] = src[k].reshape(h, w, c).astype(f32)
            pad[0, 8 : 8 + w, :] = rims[0:w]
            pad[1 : h + 1, 8 + w : 9 + w, :] = rims[w : w + h].reshape(h, 1, c)
            pad[h + 1, 8 : 8 + w, :] = rims[w + h : 2 * w + h]
            pad[1 : h + 1, 7:8, :] = rims[2 * w + h :].reshape(h, 1, c)
            for b in range(3):
                x3[k, :, :, b * c : (b + 1) * c] = pad[:, 7 + b : 7 + b + w, :].astype(bf16)
        pre = None
        for a in range(3):
            part = mm(
                x3[pl.ds(k0, G), a : a + h].reshape(G * h * w, 3 * c),
                w_ref[3 * a * c : 3 * (a + 1) * c, :],
            )
            pre = part if pre is None else pre + part
        s = 1.0 / (1.0 + jnp.exp(-pre))
        act = pre * s
        slope[pl.ds(k0, G)] = (s + act * (1.0 - s)).reshape(G, h * w, c)
        return act.astype(bf16)

    def conv_first(self, u):
        act = self.conv(u, self.x, self.x3_one, self.w1, self.d_one)
        cells = self.h * self.w
        for g in range(self.G):
            self.act_one[u * self.G + g] = act[g * cells : (g + 1) * cells]

    def cut_act(self, m):
        h, w, c = self.h, self.w, self.c

        def one(i, carry):
            self.field[...] = self.act_one[m * self.T + i].astype(f32).reshape(h, w, c)
            self.cut(self.edges_a[m], i)
            return carry

        lax.fori_loop(0, self.T, one, 0)

    def go(self, u, j):
        to = (self.member + j) % self.Z
        return rcopy(
            self.packed.at[u, to],
            self.came.at[u, j],
            self.ssem.at[0, u, j],
            self.ssem.at[1, u, j],
            member=to,
        )

    def home(self, i, j, here=False):
        back = (self.member + j) % self.Z if here else self.member
        return rcopy(
            self.slopes.at[i, j],
            self.back.at[i, back],
            self.ssem.at[2, i, j],
            self.ssem.at[3, i, j],
            member=(self.member + self.Z - j) % self.Z,
        )

    def conv_last(self, u):
        act = self.conv(u, self.act_one, self.x3_two, self.w2, self.d_two)
        G, cells, part = self.G, self.h * self.w, self.part
        outs = []
        for g in range(G):
            own = act[g * cells : (g + 1) * cells]
            self.act_two[u * G + g] = own
            outs.append(mm(self.head_t[0 : self.V, :], own, NT).astype(bf16))
        for q in range(self.Z):
            cols = [o[:, q * part : (q + 1) * part] for o in outs]
            self.packed[u, q] = jnp.concatenate(cols, axis=1) if G > 1 else cols[0]
        for j in range(1, self.Z):
            self.go(u, j).start()


    def score(self, p):
        ensemble = self.H * self.Z
        for m in range(self.H):
            for j in range(1, self.Z):
                self.go(m * self.P + p, j).wait_recv()
        rows = 16 if self.V % 16 == 0 else self.V
        for r in range(0, self.V, rows):
            at = slice(r, r + rows)
            o = self.obs_wide[p, at, :]
            names = [(m, j) for j in range(self.Z) for m in range(self.H)]
            vals = []
            for m, j in names:
                u = m * self.P + p
                v = self.packed[u, self.member, at, :] if j == 0 else self.came[u, j, at, :]
                vals.append(v.astype(f32))
            paired = [None] * len(vals)
            for a in range(len(vals)):
                for b in range(a + 1, len(vals)):
                    t = g_of(vals[a] - vals[b])
                    paired[a] = t if paired[a] is None else paired[a] + t
                    paired[b] = -t if paired[b] is None else paired[b] - t
            for (m, j), v, t in zip(names, vals, paired):
                i = p * self.H + m
                s = (g_of(v - o) / ensemble - t / (ensemble * ensemble)) / self.h
                if j == 0:
                    self.back[i, self.member, at, :] = s.astype(bf16)
                else:
                    self.slopes[i, j, at, :] = s.astype(bf16)
        for m in range(self.H):
            for j in range(1, self.Z):
                self.home(p * self.H + m, j).start()


    def prepare_back(self):
        c = self.c
        for a in range(3):
            for b in range(3):
                tap = self.w2[(3 * a + b) * c : (3 * a + b + 1) * c, :]
                self.va[a, :, b * c : (b + 1) * c] = tap
                if b == 0:
                    self.vb[0, :, a * c : (a + 1) * c] = tap
                if b == 2:
                    self.vb[1, :, a * c : (a + 1) * c] = tap
        self.hg[...] = jnp.zeros_like(self.hg)
        self.pad2[...] = jnp.zeros_like(self.pad2)

    def lanes(self, k):
        cells = self.h * self.w
        return pl.ds(pl.multiple_of(k * cells, cells), cells)

    def backward(self, i):
        h, w, c, G, H, part = self.h, self.w, self.c, self.G, self.H, self.part
        p = i // H
        m = i - p * H
        u = m * self.P + p
        for j in range(1, self.Z):
            self.home(i, j, here=True).wait_recv()
        pad = self.pad2
        for g in range(G):
            k = u * G + g
            slope_out = jnp.concatenate(
                [self.back[i, q][:, g * part : (g + 1) * part] for q in range(self.Z)], axis=1
            )
            self.hg[0 : self.V, :] += mm(slope_out, self.act_two[k])
            back = mm(slope_out, self.head_t[0 : self.V, :], TN)
            slope = (back * self.d_two[k]).astype(bf16)
            self.turned[:, self.lanes(k)] = slope.T
            pad[2 : h + 2, 8 : 8 + w, :] = slope.astype(f32).reshape(h, w, c)
            for b in range(3):
                self.s3[g, :, :, b * c : (b + 1) * c] = pad[:, 9 - b : 9 - b + w, :].astype(bf16)
            left = pad[:, 8:9, :].reshape(h + 4, c)
            right = pad[:, 7 + w : 8 + w, :].reshape(h + 4, c)
            for a in range(3):
                self.cols[0, g, :, a * c : (a + 1) * c] = left[3 - a : 3 - a + h].astype(bf16)
                self.cols[1, g, :, a * c : (a + 1) * c] = right[3 - a : 3 - a + h].astype(bf16)
        full = None
        for a in range(3):
            lhs = self.s3[:, 2 - a : 4 - a + h].reshape(G * (h + 2) * w, 3 * c)
            one = mm(lhs, self.va[a], NT)
            full = one if full is None else full + one
        full = full.reshape(G, h + 2, w, c).astype(bf16)
        self.inner[pl.ds(u * G, G)] = full[:, 1 : h + 1]
        lefts = mm(self.cols[0].reshape(G * h, 3 * c), self.vb[0], NT).astype(bf16)
        rights = mm(self.cols[1].reshape(G * h, 3 * c), self.vb[1], NT).astype(bf16)
        for g in range(G):
            at = (i * G + g) * 4
            sides = (
                full[g, 0],
                rights[g * h : (g + 1) * h],
                full[g, h + 1],
                lefts[g * h : (g + 1) * h],
            )
            for a in range(4):
                self.borders[self.face, at + a] = sides[a]

    def rims_back(self, m):
        G = self.G

        def one(i, carry):
            sides = []
            for a in range(4):
                at = i * 4 + a
                slot = self.at_slot[at]
                unit = slot // G
                j = (m * G + slot - unit * G) * 4 + self.at_side[at]
                sides.append(self.borders[self.at_face[at], unit * (self.H * G * 4) + j])
            self.rims[m * self.T + i] = mm(self.turn[i], jnp.concatenate(sides, axis=0))
            return carry

        lax.fori_loop(0, self.T, one, 0, unroll=True)

    def slope_first(self, k):
        h, w, c = self.h, self.w, self.c
        rims, field = self.rims[k], self.field
        field[...] = self.inner[k].astype(f32)
        field[0] += rims[0:w]
        field[:, w - 1 : w, :] += rims[w : w + h].reshape(h, 1, c)
        field[h - 1] += rims[w + h : 2 * w + h]
        field[:, 0:1, :] += rims[2 * w + h :].reshape(h, 1, c)
        slope = (field[...].reshape(h * w, c) * self.d_one[k]).astype(bf16)
        self.turned[:, self.lanes(k)] = slope.T

    def products(self, kb, x3):
        h, w, c, K = self.h, self.w, self.c, self.K
        cells = h * w
        at = pl.ds(pl.multiple_of(kb * K * cells, K * cells), K * cells)
        for a in range(3):
            rhs = x3[pl.ds(kb * K, K), a : a + h].reshape(K * cells, 3 * c)
            self.acc[a] += mm(self.turned[:, at], rhs)

    def turn_out(self, ref):
        c = self.c
        for a in range(3):
            for b in range(3):
                put_rows(ref, (3 * a + b) * c, self.acc[a, :, b * c : (b + 1) * c].T)
        self.acc[...] = jnp.zeros_like(self.acc)


def hooked(steps, body, before=None, after=None):
    before, after = before or {}, after or {}

    def one(i, carry):
        for s, todo in sorted(before.items()):
            pl.when(i == s)(todo)
        body(i)
        for s, todo in sorted(after.items()):
            pl.when(i == s)(todo)
        return carry

    lax.fori_loop(0, steps, one, 0)


def merge(*items):
    out = {}
    for at, todo in items:
        out.setdefault(at, []).append(todo)

    def run(todos):
        def go():
            for t in todos:
                t()

        return go

    return {at: run(todos) for at, todos in out.items()}


def step_kernel(dims, names, *refs):
    s = Step(dims, dict(zip(names, refs)))
    chips, members, H, PU = s.chips, s.Z, s.H, s.P
    gsem = s.gsem
    s.edges_x = [getattr(s, f"edges_x{m}") for m in range(H)]
    s.edges_a = [getattr(s, f"edges_a{m}") for m in range(H)]
    w1, w2, heads = [
        getattr(s, name + "_apart") if hasattr(s, name + "_apart") else getattr(s, name)
        for name in ("w1", "w2", "heads")
    ]

    def settle(name, rows):
        if hasattr(s, name + "_apart"):
            apart, whole = getattr(s, name + "_apart"), getattr(s, name)
            for d in range(apart.shape[0]):
                whole[d * rows : (d + 1) * rows, :] = apart[d]

    lw1 = LineGather(s.w_own.at[0], w1, s.rows, members, s.lsem.at[0])
    lw2 = LineGather(s.w_own.at[1], w2, s.rows, members, s.lsem.at[1])
    lhd = LineGather(s.head_own, heads, s.hrows, members, s.lsem.at[2])
    gw1 = gather_rows(w1, s.rows, members, chips, gsem.at[0])
    gw2 = gather_rows(w2, s.rows, members, chips, gsem.at[1])
    ghd = gather_rows(heads, s.hrows, members, chips, gsem.at[2])
    sides, share = s.T * 4, H * s.G * 4
    gx = [gather_edges(s.edges_x[m], 0, sides, chips, gsem.at[3 + m]) for m in range(H)]
    ga = [gather_edges(s.edges_a[m], 0, sides, chips, gsem.at[3 + H + m]) for m in range(H)]
    gb = [
        gather_edges(s.borders, p * share, share, chips, gsem.at[3 + 2 * H + p])
        for p in range(PU)
    ]

    for layer in range(2):
        s.w_own[layer] = s.weights[:, layer, :]
    s.head_own[...] = jnp.zeros_like(s.head_own)
    s.head_own[:, 0 : s.V] = s.head[...]
    s.cut_input(0)
    greet(chips, members)
    lw1.start()
    gx[0].start()
    for m in range(1, H):
        s.cut_input(m)
    s.pad[...] = jnp.zeros_like(s.pad)
    lw1.wait()
    gw1.start()
    lw2.start()
    lhd.start()
    s.tables()
    s.turn_inputs()
    gx[0].relay_first()
    gw1.relay_first()
    gx[0].relay_rest()
    gw1.relay_rest()
    for m in range(1, H):
        gx[m].start()
    lw2.wait()
    lhd.wait()
    gw2.start()
    ghd.start()
    gw1.finish()
    settle("w1", s.rows)

    last = H * PU - 1

    def ready_x(m):
        gx[m].finish()
        s.rims_from(s.edges_x[m], m)

    def send_a(m):
        s.cut_act(m)
        ga[m].start()

    def ready_a(m):
        ga[m].finish()
        s.rims_from(s.edges_a[m], m)

    before = {m * PU: functools.partial(ready_x, m) for m in range(H)}
    after = []
    for m in range(1, H):
        after.append((max(m * PU - 3, 0), gx[m].relay_first))
        after.append((m * PU - 2 if PU > 1 else 0, gx[m].relay_rest))
    for m in range(H - 1):
        after.append(((m + 1) * PU - 1, functools.partial(send_a, m)))
    after.append((min(PU, last), gw2.relay_first))
    after.append((min(PU, last), ghd.relay_first))
    after.append((min(PU + 1, last), gw2.relay_rest))
    after.append((min(PU + 1, last), ghd.relay_rest))
    for m in range(H - 1):
        after.append((min((m + 1) * PU + 2, last), ga[m].relay_first))
    hooked(H * PU, s.conv_first, before, merge(*after))
    s.cut_act(H - 1)
    for m in range(H - 1):
        ga[m].relay_rest()
    ga[H - 1].start()
    gw2.finish()
    ghd.finish()
    settle("w2", s.rows)
    settle("heads", s.hrows)
    s.head_t[...] = s.heads[...].astype(f32).T.astype(bf16)

    before = {m * PU: functools.partial(ready_a, m) for m in range(H)}
    after = [
        (max((H - 1) * PU - 2, 0), ga[H - 1].relay_first),
        (max((H - 1) * PU - 1, 0), ga[H - 1].relay_rest),
    ]
    hooked(H * PU, s.conv_last, before, merge(*after))
    s.prepare_back()

    lax.fori_loop(0, PU, lambda p, carry: (s.score(p), carry)[1], 0)
    after = []
    late = []
    total = H * PU
    for p in range(PU):
        at = (p + 1) * H - 1
        after.append((at, gb[p].start))
        for step, todo in ((at + 2, gb[p].relay_first), (at + 4, gb[p].relay_rest)):
            if step < total:
                after.append((step, todo))
            else:
                late.append((min(step - total, s.n // s.K - 1), todo))
    hooked(total, s.backward, None, merge(*after))

    s.acc[...] = jnp.zeros_like(s.acc)
    hooked(s.n // s.K, lambda kb: s.products(kb, s.x3_two), None, merge(*late))
    s_two = Scatter(s.two, chips, members, [getattr(s, f"t{i}") for i in range(10)], s.csem.at[0])
    s_head = Scatter(s.hg_t, chips, members, [getattr(s, f"h{i}") for i in range(6)], s.csem.at[1])
    s_one = Scatter(s.one, chips, members, [getattr(s, f"o{i}") for i in range(10)], s.csem.at[2])
    s.turn_out(s.two)
    put_rows(s.hg_t, 0, s.hg[...].T)
    s_two.core_start()
    s_head.core_start()

    for p in range(PU):
        gb[p].finish()
    for m in range(H):
        s.rims_back(m)
    s_two.core_done()
    s_head.core_done()
    lax.fori_loop(0, s.n, lambda k, carry: (s.slope_first(k), carry)[1], 0)
    hooked(s.n // s.K, lambda kb: s.products(kb, s.x3_one))
    s.turn_out(s.one)
    s_one.core_start()
    s_two.chip_done()
    s_head.chip_done()
    s_one.core_done()
    s.grads[:, 1, :] = s_two.line_done()
    s.head_out[...] = s_head.line_done()
    s_one.chip_done()
    s.grads[:, 0, :] = s_one.line_done()
    for scatter in (s_two, s_head, s_one):
        scatter.finish()
    for u in range(H * PU):
        for j in range(1, members):
            s.go(u, j).wait_send()
            s.home(u, j).wait_send()


def shards(faces, zs, features, observed, conv_weights, head_weight, adjacency, placement_map):
    H, T, h, w, c = features.shape
    n = H * T
    V = head_weight.shape[1]
    rows, hrows = conv_weights.shape[0], head_weight.shape[0]
    lanes = -(-V // 128) * 128
    chips = faces // 2
    G = 2 if T % 2 == 0 else 1
    PU = T // G
    K = 4 if n % 4 == 0 else (2 if n % 2 == 0 else 1)
    part = observed.shape[-1]
    cells = h * w
    dims = dict(
        H=H, T=T, h=h, w=w, c=c, n=n, V=V, rows=rows, hrows=hrows, chips=chips, Z=zs, G=G, P=PU,
        K=K, part=part,
    )
    side = 4 * w
    total_rows = rows * faces * zs
    total_heads = hrows * faces * zs
    scratch = {
        "at_face": SMEM((T * 4,), jnp.int32),
        "at_slot": SMEM((T * 4,), jnp.int32),
        "at_side": SMEM((T * 4,), jnp.int32),
        "turn": VMEM((T, side, side), bf16),
        "obs_wide": VMEM((PU, V, G * part), f32),
        "w_own": VMEM((2, rows, c), bf16),
        "rims": VMEM((n, side, c), f32),
        "field": VMEM((h, w, c), f32),
        "pad": VMEM((h + 2, w + 16, c), f32),
        "pad2": VMEM((h + 4, w + 16, c), f32),
        "head_own": VMEM((hrows, lanes), bf16),
        "w1": VMEM((total_rows, c), bf16),
        "w2": VMEM((total_rows, c), bf16),
        "heads": VMEM((total_heads, lanes), bf16),
        "head_t": VMEM((lanes, total_heads), bf16),
        "x3_one": VMEM((n, h + 2, w, 3 * c), bf16),
        "x3_two": VMEM((n, h + 2, w, 3 * c), bf16),
        "d_one": VMEM((n, cells, c), f32),
        "d_two": VMEM((n, cells, c), f32),
        "act_one": VMEM((n, cells, c), bf16),
        "act_two": VMEM((n, cells, c), bf16),
        "packed": VMEM((H * PU, zs, V, G * part), bf16),
        "came": VMEM((H * PU, zs, V, G * part), bf16),
        "slopes": VMEM((H * PU, zs, V, G * part), bf16),
        "back": VMEM((H * PU, zs, V, G * part), bf16),
        "va": VMEM((3, c, 3 * c), bf16),
        "vb": VMEM((2, c, 3 * c), bf16),
        "s3": VMEM((G, h + 4, w, 3 * c), bf16),
        "cols": VMEM((2, G, h, 3 * c), bf16),
        "inner": VMEM((n, h, w, c), bf16),
        "turned": VMEM((c, n * cells), bf16),
        "acc": VMEM((3, c, 3 * c), f32),
        "hg": VMEM((lanes, c), f32),
        "hg_t": VMEM((faces * zs, hrows, lanes), f32),
        "one": VMEM((faces * zs, rows, c), f32),
        "two": VMEM((faces * zs, rows, c), f32),
        "borders": VMEM((faces, PU * H * G * 4, w, c), bf16),
    }
    for m in range(H):
        scratch[f"edges_x{m}"] = VMEM((faces, T * 4, w, c), bf16)
        scratch[f"edges_a{m}"] = VMEM((faces, T * 4, w, c), bf16)
    for name, r, lane, code in (("t", rows, c, True), ("h", hrows, lanes, False), ("o", rows, c, True)):
        for i, v in enumerate(scatter_scratch(chips, zs, r, lane, code)):
            scratch[f"{name}{i}"] = v
    if rows % 16:
        for name in ("w1_apart", "w2_apart"):
            scratch[name] = VMEM((faces * zs, rows, c), bf16)
    if hrows % 16:
        scratch["heads_apart"] = VMEM((faces * zs, hrows, lanes), bf16)
    dma = pltpu.SemaphoreType.DMA
    scratch["gsem"] = dma((3 + 2 * H + PU, 4, chips + 3))
    scratch["lsem"] = dma((3, 2, zs))
    scratch["ssem"] = dma((4, H * PU, zs))
    scratch["csem"] = dma((3, 10, max(chips, zs)))
    vmem = pl.BlockSpec(memory_space=VMEM)
    smem = pl.BlockSpec(memory_space=SMEM)
    ins = ["place", "glue", "x", "obs", "weights", "head"]
    outs = ["grads", "head_out"]
    grads, head_out = pl.pallas_call(
        functools.partial(step_kernel, dims, ins + outs + list(scratch)),
        out_shape=[
            jax.ShapeDtypeStruct((rows, 2, c), f32),
            jax.ShapeDtypeStruct((hrows, lanes), f32),
        ],
        in_specs=[smem, smem] + [vmem] * 4,
        out_specs=[vmem] * 2,
        scratch_shapes=list(scratch.values()),
        compiler_params=pltpu.CompilerParams(
            collective_id=1, has_side_effects=True, vmem_limit_bytes=LIMIT
        ),
        name="step",
    )(
        placement_map,
        adjacency.transpose(2, 1, 0),
        features.reshape(n, cells, c),
        observed.transpose(0, 2, 1),
        conv_weights,
        head_weight,
    )
    return grads, head_out[:, :V]


def solution(mesh):
    in_specs = (
        P("member", "face", None, None, None),
        P("face", None, "member"),
        P(("face", "member"), None, None),
        P(("face", "member"), None),
        P(),
        P(),
    )
    out_specs = (P(("face", "member"), None, None), P(("face", "member"), None))
    body = functools.partial(shards, mesh.shape["face"], mesh.shape["member"])
    return jax.shard_map(body, mesh=mesh, in_specs=in_specs, out_specs=out_specs, check_vma=False)
```

```python
import functools

import jax
import jax.numpy as jnp
from jax import lax
from jax.experimental import pallas as pl
from jax.experimental.pallas import tpu as pltpu
from jax.sharding import PartitionSpec as P

smooth_sq = 0.0625
MESH = pl.DeviceIdType.MESH
VMEM = pltpu.VMEM
SMEM = pltpu.SMEM
f32 = jnp.float32
bf16 = jnp.bfloat16
i16 = jnp.int16
LIMIT = 62 * 1024 * 1024
TOP = 32767.0
NT = (((1,), (1,)), ((), ()))
TN = (((0,), (0,)), ((), ()))
NN = (((1,), (0,)), ((), ()))


def mm(a, b, dims=NN):
    return lax.dot_general(a, b, dims, preferred_element_type=f32)


def rcopy(src, dst, send, recv, **where):
    return pltpu.make_async_remote_copy(
        src_ref=src, dst_ref=dst, send_sem=send, recv_sem=recv, device_id=where, device_id_type=MESH
    )


def greet(chips, members):
    face = lax.axis_index("face")
    member = lax.axis_index("member")
    core = face % 2
    chip = face // 2
    barrier = pltpu.get_barrier_semaphore()
    pl.semaphore_signal(
        barrier, inc=1, device_id={"face": chip * 2 + 1 - core}, device_id_type=MESH
    )
    for j in range(1, chips):
        pl.semaphore_signal(
            barrier,
            inc=1,
            device_id={"face": ((chip + j) % chips) * 2 + core},
            device_id_type=MESH,
        )
    for j in range(1, members):
        pl.semaphore_signal(
            barrier, inc=1, device_id={"member": (member + j) % members}, device_id_type=MESH
        )
    pl.semaphore_wait(barrier, chips + members - 1)


class FaceGather:
    def __init__(self, at, chips, sems):
        self.at, self.chips, self.sems = at, chips, sems
        face = lax.axis_index("face")
        self.face, self.core, self.chip = face, face % 2, face // 2
        self.partner = self.chip * 2 + 1 - self.core

    def direct(self, j):
        mine = self.at(self.face, None)
        return rcopy(
            mine,
            mine,
            self.sems.at[0, j],
            self.sems.at[1, j],
            face=((self.chip + j) % self.chips) * 2 + self.core,
        )

    def forward(self, j):
        block = self.at(((self.chip + self.chips - j) % self.chips) * 2 + self.core, None)
        return rcopy(block, block, self.sems.at[2, j], self.sems.at[3, j], face=self.partner)

    def start(self):
        for j in range(1, self.chips):
            self.direct(j).start()
        self.forward(0).start()

    def relay_first(self):
        pass

    def relay_rest(self):
        for j in range(1, self.chips):
            self.direct(j).wait_recv()
            self.forward(j).start()

    def finish(self):
        for j in range(1, self.chips):
            self.direct(j).wait_send()
        for j in range(self.chips):
            self.forward(j).wait()


class SquareGather:
    def __init__(self, at, chips, sems):
        self.at, self.sems = at, sems
        face = lax.axis_index("face")
        core, chip = face % 2, face // 2
        col, row = chip % 2, chip // 2
        self.face = face
        self.partner = chip * 2 + 1 - core
        self.beside = (row * 2 + 1 - col) * 2 + core
        self.below = ((1 - row) * 2 + col) * 2 + core
        self.across = ((1 - row) * 2 + 1 - col) * 2 + core

    def direct(self, k):
        to = (self.beside, self.beside, self.below, self.below, self.below, self.beside)[k]
        block = (self.face,) * 4 + (self.beside, self.below)
        ref = self.at(block[k], (0, 1, 1, 0, 0, 1)[k])
        return rcopy(ref, ref, self.sems.at[0, k], self.sems.at[1, k], face=to)

    def forward(self, k):
        if k == 6:
            ref = self.at(self.face, None)
        else:
            block = (
                self.beside,
                self.beside,
                self.below,
                self.below,
                self.across,
                self.across,
            )
            ref = self.at(block[k], (0, 1, 1, 0, 0, 1)[k])
        return rcopy(ref, ref, self.sems.at[2, k], self.sems.at[3, k], face=self.partner)

    def start(self):
        for k in (0, 2, 1, 3):
            self.direct(k).start()
        self.forward(6).start()

    def relay_first(self):
        for k, onward in ((0, 4), (2, 5)):
            self.direct(k).wait_recv()
            self.direct(onward).start()
            self.forward(k).start()

    def relay_rest(self):
        for k in (1, 3, 4, 5):
            self.direct(k).wait_recv()
            self.forward(k).start()

    def finish(self):
        for k in range(6):
            self.direct(k).wait_send()
        for k in range(7):
            self.forward(k).wait()


def units(ref, rows, start, count):
    if len(ref.shape) == 3:
        return ref.at[pl.ds(start, count)] if count > 1 else ref.at[start]
    return ref.at[pl.ds(pl.multiple_of(start * rows, rows), count * rows)]


def gather_rows(ref, rows, members, chips, sems):
    def at(block, part):
        if part is None:
            return units(ref, rows, block * members, members)
        half = members // 2
        return units(ref, rows, block * members + part * half, half)

    return (SquareGather if chips == 4 and members % 2 == 0 else FaceGather)(at, chips, sems)


def gather_edges(ref, start, count, chips, sems):
    def at(block, part):
        if part is None:
            return ref.at[block, pl.ds(start, count)]
        half = count // 2
        return ref.at[block, pl.ds(start + part * half, half)]

    return (SquareGather if chips == 4 and count % 2 == 0 else FaceGather)(at, chips, sems)


class LineGather:
    def __init__(self, src, ref, rows, members, sems):
        self.src, self.ref, self.rows, self.members, self.sems = src, ref, rows, members, sems
        self.face, self.member = lax.axis_index("face"), lax.axis_index("member")

    def at(self, member):
        return units(self.ref, self.rows, self.face * self.members + member, 1)

    def own(self):
        return pltpu.make_async_copy(self.src, self.at(self.member), self.sems.at[0, 0])

    def send(self, j):
        to = (self.member + j) % self.members
        return rcopy(
            self.src, self.at(self.member), self.sems.at[0, j], self.sems.at[1, j], member=to
        )

    def came(self, j):
        origin = (self.member + self.members - j) % self.members
        return rcopy(
            self.src, self.at(origin), self.sems.at[0, j], self.sems.at[1, j], member=origin
        )

    def start(self):
        self.own().start()
        for j in range(1, self.members):
            self.send(j).start()

    def wait(self):
        self.own().wait()
        for j in range(1, self.members):
            self.came(j).wait_recv()
            self.send(j).wait_send()


class PlaneLine:
    def __init__(self, src, ref, chips, members, sems):
        self.src, self.ref, self.chips, self.members, self.sems = src, ref, chips, members, sems
        self.member = lax.axis_index("member")
        face = lax.axis_index("face")
        self.core, self.chip = face % 2, face // 2
        self.partner = self.chip * 2 + 1 - self.core

    def mine(self):
        return self.ref.at[(self.member * 2 + self.core) * self.chips + self.chip]

    def own(self):
        return pltpu.make_async_copy(self.src, self.mine(), self.sems.at[0, 0])

    def plane(self, j):
        to = ((self.chip + j) % self.chips) * 2 + self.core
        return rcopy(self.src, self.mine(), self.sems.at[0, j], self.sems.at[1, j], face=to)

    def group(self, j):
        member = (self.member + self.members - j) % self.members
        return self.ref.at[pl.ds((member * 2 + self.core) * self.chips, self.chips)]

    def line(self, j):
        to = (self.member + j) % self.members
        ref = self.group(0)
        return rcopy(ref, ref, self.sems.at[2, j], self.sems.at[3, j], member=to)

    def cross(self, j):
        ref = self.group(j)
        return rcopy(ref, ref, self.sems.at[4, j], self.sems.at[5, j], face=self.partner)

    def start(self):
        self.own().start()
        for j in range(1, self.chips):
            self.plane(j).start()

    def relay_first(self):
        self.own().wait()
        for j in range(1, self.chips):
            self.plane(j).wait_recv()
        for j in range(1, self.members):
            self.line(j).start()
        self.cross(0).start()

    def relay_rest(self):
        for j in range(1, self.members):
            self.line(j).wait_recv()
            self.cross(j).start()

    def finish(self):
        for j in range(1, self.chips):
            self.plane(j).wait_send()
        for j in range(1, self.members):
            self.line(j).wait_send()
        for j in range(self.members):
            self.cross(j).wait()


def coded(v):
    axes = tuple(range(v.ndim - 1))
    most = jnp.max(jnp.abs(v), axis=axes, keepdims=True)
    code = jnp.round(v * (TOP / jnp.maximum(most, 1e-33))).astype(jnp.int32).astype(i16)
    most = most.reshape(1, v.shape[-1])
    return code, jnp.broadcast_to(most * (1.0 / TOP), (8, v.shape[-1]))


def decoded(code, scale):
    return code.astype(jnp.int32).astype(f32) * scale[0:1, :]


class Scatter:
    def __init__(self, g, chips, members, scratch, sems):
        self.g, self.chips, self.members = g, chips, members
        self.fromcore, self.acc, self.out1, self.in1, self.out2, self.in2 = scratch[:6]
        self.sc = scratch[6:]
        self.sems = sems
        face = lax.axis_index("face")
        self.member = lax.axis_index("member")
        self.core, self.chip = face % 2, face // 2
        self.partner = self.chip * 2 + 1 - self.core
        self.order = list(range(1, chips)) + [0]

    def part(self, chip, core):
        return pl.ds((chip * 2 + core) * self.members, self.members)

    def there(self, j):
        return (self.chip + j) % self.chips

    def core_copy(self, j):
        return rcopy(
            self.g.at[self.part(self.there(j), 1 - self.core)],
            self.fromcore.at[j],
            self.sems.at[0, j],
            self.sems.at[1, j],
            face=self.partner,
        )

    def copies(self, first, boxes, j, **to):
        s = self.sems
        return [
            rcopy(a.at[j], b.at[j], s.at[i, j], s.at[i + 1, j], **to)
            for i, (a, b) in zip((first, first + 2), boxes)
        ]

    def chip_copies(self, j):
        boxes = [(self.out1, self.in1)] + ([(self.sc[0], self.sc[1])] if self.sc else [])
        return self.copies(2, boxes, j, face=self.there(j) * 2 + self.core)

    def line_copies(self, j):
        boxes = [(self.out2, self.in2)] + ([(self.sc[2], self.sc[3])] if self.sc else [])
        return self.copies(6, boxes, j, member=(self.member + j) % self.members)

    def core_start(self):
        for j in self.order:
            self.core_copy(j).start()

    def core_done(self):
        for j in self.order:
            self.core_copy(j).wait_recv()
            total = self.g[self.part(self.there(j), self.core)] + self.fromcore[j]
            if j == 0:
                self.acc[...] = total
                continue
            if self.sc:
                self.out1[j], self.sc[0][j] = coded(total)
            else:
                self.out1[j] = total
            for c in self.chip_copies(j):
                c.start()

    def summed(self, to):
        v = self.acc[to]
        for i in range(1, self.chips):
            piece = self.in1[i, to]
            v = v + (decoded(piece, self.sc[1][i]) if self.sc else piece)
        return v

    def chip_done(self):
        for j in range(1, self.chips):
            for c in self.chip_copies(j):
                c.wait_recv()
        for j in range(1, self.members):
            v = self.summed((self.member + j) % self.members)
            if self.sc:
                self.out2[j], self.sc[2][j] = coded(v)
            else:
                self.out2[j] = v
            for c in self.line_copies(j):
                c.start()

    def line_done(self):
        total = self.summed(self.member)
        for j in range(1, self.members):
            for c in self.line_copies(j):
                c.wait_recv()
            piece = self.in2[j]
            total = total + (decoded(piece, self.sc[3][j]) if self.sc else piece)
        return total

    def finish(self):
        for j in range(self.chips):
            self.core_copy(j).wait_send()
        for j in range(1, self.chips):
            for c in self.chip_copies(j):
                c.wait_send()
        for j in range(1, self.members):
            for c in self.line_copies(j):
                c.wait_send()


def scatter_scratch(chips, members, rows, lanes, code):
    kind = i16 if code else f32
    out = [
        VMEM((chips, members, rows, lanes), f32),
        VMEM((members, rows, lanes), f32),
        VMEM((chips, members, rows, lanes), kind),
        VMEM((chips, members, rows, lanes), kind),
        VMEM((members, rows, lanes), kind),
        VMEM((members, rows, lanes), kind),
    ]
    if code:
        out += [VMEM((chips, 8, lanes), f32)] * 2 + [VMEM((members, 8, lanes), f32)] * 2
    return out


def put_rows(ref, first, v):
    rows, done = ref.shape[1], 0
    while done < v.shape[0]:
        block, at = divmod(first + done, rows)
        size = min(rows - at, v.shape[0] - done)
        ref[block, at : at + size, :] = v[done : done + size]
        done += size


def sides_of(field):
    h, w, c = field.shape
    return [
        field[0],
        field[:, w - 1 : w, :].reshape(h, c),
        field[h - 1],
        field[:, 0:1, :].reshape(h, c),
    ]


def g_of(v):
    return v * lax.rsqrt(v * v + smooth_sq)


class Step:
    def __init__(self, dims, refs):
        self.__dict__.update(dims)
        self.__dict__.update(refs)
        face = lax.axis_index("face")
        self.face, self.member = face, lax.axis_index("member")


    def tables(self):
        first = self.face * self.T
        total = self.place.shape[0]

        def fill(i, carry):
            tile = self.place[first + i]
            for a in range(4):
                want = self.glue[0, a, tile]

                def look(s, slot):
                    return jnp.where(self.place[s] == want, s, slot)

                slot = lax.fori_loop(0, total, look, jnp.int32(0), unroll=8)
                owner = slot // self.T
                self.at_face[i * 4 + a] = owner
                self.at_slot[i * 4 + a] = slot - owner * self.T
                self.at_side[i * 4 + a] = self.glue[1, a, tile]
            size = 4 * self.w
            row = lax.broadcasted_iota(jnp.int32, (size, size), 0)
            col = lax.broadcasted_iota(jnp.int32, (size, size), 1)
            side = row // self.w
            at = row - side * self.w
            flag = jnp.zeros((size, size), jnp.int32)
            for a in range(4):
                flag = jnp.where(side == a, self.glue[2, a, tile], flag)
            target = side * self.w + jnp.where(flag == 1, self.w - 1 - at, at)
            self.turn[i] = jnp.where(col == target, 1.0, 0.0).astype(bf16)
            return carry

        lax.fori_loop(0, self.T, fill, 0)

    def rims_from(self, box, m):
        def one(i, carry):
            cat = jnp.concatenate(
                [
                    box[self.at_face[i * 4 + a], self.at_slot[i * 4 + a] * 4 + self.at_side[i * 4 + a]]
                    for a in range(4)
                ],
                axis=0,
            )
            self.rims[m * self.T + i] = mm(self.turn[i], cat)
            return carry

        lax.fori_loop(0, self.T, one, 0, unroll=True)

    def turn_inputs(self):
        for p in range(self.P):
            o = [self.obs[p * self.G + g].astype(f32).T for g in range(self.G)]
            self.obs_wide[p] = jnp.concatenate(o, axis=1) if self.G > 1 else o[0]

    def cut(self, box, i):
        for a, v in enumerate(sides_of(self.field)):
            box[self.face, i * 4 + a] = v.astype(bf16)

    def cut_input(self, m):
        def one(i, carry):
            v = self.x[m * self.T + i].astype(f32)
            self.field[...] = v.reshape(self.h, self.w, self.c)
            self.cut(self.edges_x[m], i)
            return carry

        lax.fori_loop(0, self.T, one, 0)


    def conv(self, u, src, x3, w_ref, slope):
        h, w, c, G = self.h, self.w, self.c, self.G
        k0 = u * G
        pad = self.pad
        for g in range(G):
            k = k0 + g
            rims = self.rims[k]
            pad[1 : h + 1, 8 : 8 + w, :] = src[k].reshape(h, w, c).astype(f32)
            pad[0, 8 : 8 + w, :] = rims[0:w]
            pad[1 : h + 1, 8 + w : 9 + w, :] = rims[w : w + h].reshape(h, 1, c)
            pad[h + 1, 8 : 8 + w, :] = rims[w + h : 2 * w + h]
            pad[1 : h + 1, 7:8, :] = rims[2 * w + h :].reshape(h, 1, c)
            for b in range(3):
                x3[k, :, :, b * c : (b + 1) * c] = pad[:, 7 + b : 7 + b + w, :].astype(bf16)
        pre = None
        for a in range(3):
            part = mm(
                x3[pl.ds(k0, G), a : a + h].reshape(G * h * w, 3 * c),
                w_ref[3 * a * c : 3 * (a + 1) * c, :],
            )
            pre = part if pre is None else pre + part
        s = 1.0 / (1.0 + jnp.exp(-pre))
        act = pre * s
        slope[pl.ds(k0, G)] = (s + act * (1.0 - s)).reshape(G, h * w, c)
        return act.astype(bf16)

    def conv_first(self, u):
        act = self.conv(u, self.x, self.x3_one, self.w1, self.d_one)
        cells = self.h * self.w
        for g in range(self.G):
            self.act_one[u * self.G + g] = act[g * cells : (g + 1) * cells]

    def cut_act(self, m):
        h, w, c = self.h, self.w, self.c

        def one(i, carry):
            self.field[...] = self.act_one[m * self.T + i].astype(f32).reshape(h, w, c)
            self.cut(self.edges_a[m], i)
            return carry

        lax.fori_loop(0, self.T, one, 0)

    def go(self, u, j):
        to = (self.member + j) % self.Z
        return rcopy(
            self.packed.at[u, to],
            self.came.at[u, j],
            self.ssem.at[0, u, j],
            self.ssem.at[1, u, j],
            member=to,
        )

    def home(self, i, j, here=False):
        back = (self.member + j) % self.Z if here else self.member
        return rcopy(
            self.slopes.at[i, j],
            self.back.at[i, back],
            self.ssem.at[2, i, j],
            self.ssem.at[3, i, j],
            member=(self.member + self.Z - j) % self.Z,
        )

    def conv_last(self, u):
        act = self.conv(u, self.act_one, self.x3_two, self.w2, self.d_two)
        G, cells, part = self.G, self.h * self.w, self.part
        outs = []
        for g in range(G):
            own = act[g * cells : (g + 1) * cells]
            self.act_two[u * G + g] = own
            outs.append(mm(self.head_t[0 : self.V, :], own, NT).astype(bf16))
        for q in range(self.Z):
            cols = [o[:, q * part : (q + 1) * part] for o in outs]
            self.packed[u, q] = jnp.concatenate(cols, axis=1) if G > 1 else cols[0]
        for j in range(1, self.Z):
            self.go(u, j).start()


    def score(self, p):
        ensemble = self.H * self.Z
        for m in range(self.H):
            for j in range(1, self.Z):
                self.go(m * self.P + p, j).wait_recv()
        rows = 16 if self.V % 16 == 0 else self.V
        for r in range(0, self.V, rows):
            at = slice(r, r + rows)
            o = self.obs_wide[p, at, :]
            names = [(m, j) for j in range(self.Z) for m in range(self.H)]
            vals = []
            for m, j in names:
                u = m * self.P + p
                v = self.packed[u, self.member, at, :] if j == 0 else self.came[u, j, at, :]
                vals.append(v.astype(f32))
            paired = [None] * len(vals)
            for a in range(len(vals)):
                for b in range(a + 1, len(vals)):
                    t = g_of(vals[a] - vals[b])
                    paired[a] = t if paired[a] is None else paired[a] + t
                    paired[b] = -t if paired[b] is None else paired[b] - t
            for (m, j), v, t in zip(names, vals, paired):
                i = p * self.H + m
                s = (g_of(v - o) / ensemble - t / (ensemble * ensemble)) / self.h
                if j == 0:
                    self.back[i, self.member, at, :] = s.astype(bf16)
                else:
                    self.slopes[i, j, at, :] = s.astype(bf16)
        for m in range(self.H):
            for j in range(1, self.Z):
                self.home(p * self.H + m, j).start()


    def prepare_back(self):
        c = self.c
        for a in range(3):
            for b in range(3):
                tap = self.w2[(3 * a + b) * c : (3 * a + b + 1) * c, :]
                self.va[a, :, b * c : (b + 1) * c] = tap
                if b == 0:
                    self.vb[0, :, a * c : (a + 1) * c] = tap
                if b == 2:
                    self.vb[1, :, a * c : (a + 1) * c] = tap
        self.hg[...] = jnp.zeros_like(self.hg)
        self.pad2[...] = jnp.zeros_like(self.pad2)

    def lanes(self, k):
        cells = self.h * self.w
        return pl.ds(pl.multiple_of(k * cells, cells), cells)

    def backward(self, i):
        h, w, c, G, H, part = self.h, self.w, self.c, self.G, self.H, self.part
        p = i // H
        m = i - p * H
        u = m * self.P + p
        for j in range(1, self.Z):
            self.home(i, j, here=True).wait_recv()
        pad = self.pad2
        for g in range(G):
            k = u * G + g
            slope_out = jnp.concatenate(
                [self.back[i, q][:, g * part : (g + 1) * part] for q in range(self.Z)], axis=1
            )
            self.hg[0 : self.V, :] += mm(slope_out, self.act_two[k])
            back = mm(slope_out, self.head_t[0 : self.V, :], TN)
            slope = (back * self.d_two[k]).astype(bf16)
            self.turned[:, self.lanes(k)] = slope.T
            pad[2 : h + 2, 8 : 8 + w, :] = slope.astype(f32).reshape(h, w, c)
            for b in range(3):
                self.s3[g, :, :, b * c : (b + 1) * c] = pad[:, 9 - b : 9 - b + w, :].astype(bf16)
            left = pad[:, 8:9, :].reshape(h + 4, c)
            right = pad[:, 7 + w : 8 + w, :].reshape(h + 4, c)
            for a in range(3):
                self.cols[0, g, :, a * c : (a + 1) * c] = left[3 - a : 3 - a + h].astype(bf16)
                self.cols[1, g, :, a * c : (a + 1) * c] = right[3 - a : 3 - a + h].astype(bf16)
        full = None
        for a in range(3):
            lhs = self.s3[:, 2 - a : 4 - a + h].reshape(G * (h + 2) * w, 3 * c)
            one = mm(lhs, self.va[a], NT)
            full = one if full is None else full + one
        full = full.reshape(G, h + 2, w, c).astype(bf16)
        self.inner[pl.ds(u * G, G)] = full[:, 1 : h + 1]
        lefts = mm(self.cols[0].reshape(G * h, 3 * c), self.vb[0], NT).astype(bf16)
        rights = mm(self.cols[1].reshape(G * h, 3 * c), self.vb[1], NT).astype(bf16)
        for g in range(G):
            at = (i * G + g) * 4
            sides = (
                full[g, 0],
                rights[g * h : (g + 1) * h],
                full[g, h + 1],
                lefts[g * h : (g + 1) * h],
            )
            for a in range(4):
                self.borders[self.face, at + a] = sides[a]

    def rims_back(self, m):
        G = self.G

        def one(i, carry):
            sides = []
            for a in range(4):
                at = i * 4 + a
                slot = self.at_slot[at]
                unit = slot // G
                j = (m * G + slot - unit * G) * 4 + self.at_side[at]
                sides.append(self.borders[self.at_face[at], unit * (self.H * G * 4) + j])
            self.rims[m * self.T + i] = mm(self.turn[i], jnp.concatenate(sides, axis=0))
            return carry

        lax.fori_loop(0, self.T, one, 0, unroll=True)

    def slope_first(self, k):
        h, w, c = self.h, self.w, self.c
        rims, field = self.rims[k], self.field
        field[...] = self.inner[k].astype(f32)
        field[0] += rims[0:w]
        field[:, w - 1 : w, :] += rims[w : w + h].reshape(h, 1, c)
        field[h - 1] += rims[w + h : 2 * w + h]
        field[:, 0:1, :] += rims[2 * w + h :].reshape(h, 1, c)
        slope = (field[...].reshape(h * w, c) * self.d_one[k]).astype(bf16)
        self.turned[:, self.lanes(k)] = slope.T

    def products(self, kb, x3, cols):
        h, w, c, K = self.h, self.w, self.c, self.K
        cells = h * w
        at = pl.ds(pl.multiple_of(kb * K * cells, K * cells), K * cells)
        for a in range(3):
            rhs = x3[pl.ds(kb * K, K), a : a + h].reshape(K * cells, 3 * c)
            self.acc[a, cols, :] += mm(self.turned[cols, at], rhs)

    def turn_out(self, ref, cols):
        c = self.c
        for a in range(3):
            for b in range(3):
                put_rows(ref, (3 * a + b) * c, self.acc[a, cols, b * c : (b + 1) * c].T)


def hooked(steps, body, before=None, after=None):
    before, after = before or {}, after or {}

    def one(i, carry):
        for s, todo in sorted(before.items()):
            pl.when(i == s)(todo)
        body(i)
        for s, todo in sorted(after.items()):
            pl.when(i == s)(todo)
        return carry

    lax.fori_loop(0, steps, one, 0)


def merge(*items):
    out = {}
    for at, todo in items:
        out.setdefault(at, []).append(todo)

    def run(todos):
        def go():
            for t in todos:
                t()

        return go

    return {at: run(todos) for at, todos in out.items()}


def step_kernel(dims, names, *refs):
    s = Step(dims, dict(zip(names, refs)))
    chips, members, H, PU = s.chips, s.Z, s.H, s.P
    gsem = s.gsem
    s.edges_x = [getattr(s, f"edges_x{m}") for m in range(H)]
    s.edges_a = [getattr(s, f"edges_a{m}") for m in range(H)]
    w1 = s.w1_apart if hasattr(s, "w1_apart") else s.w1

    def settle():
        if hasattr(s, "w1_apart"):
            for d in range(chips * 2 * members):
                s.w1[d * s.rows : (d + 1) * s.rows, :] = s.w1_apart[d]

    def settle_last():
        for d in range(chips * 2 * members):
            face, member = divmod(d, members)
            at = (member * 2 + face % 2) * chips + face // 2
            s.w2[d * s.rows : (d + 1) * s.rows, :] = s.w2_apart[at]
            s.heads[d * s.hrows : (d + 1) * s.hrows, :] = s.heads_apart[at]

    lw1 = LineGather(s.w_own.at[0], w1, s.rows, members, s.lsem.at[0])
    gw1 = gather_rows(w1, s.rows, members, chips, gsem.at[0])
    later = [
        PlaneLine(s.w_own.at[1], s.w2_apart, chips, members, s.psem.at[0]),
        PlaneLine(s.head_own, s.heads_apart, chips, members, s.psem.at[1]),
    ]
    sides, share = s.T * 4, H * s.G * 4
    gx = [gather_edges(s.edges_x[m], 0, sides, chips, gsem.at[3 + m]) for m in range(H)]
    ga = [gather_edges(s.edges_a[m], 0, sides, chips, gsem.at[3 + H + m]) for m in range(H)]
    gb = [
        gather_edges(s.borders, p * share, share, chips, gsem.at[3 + 2 * H + p])
        for p in range(PU)
    ]

    for layer in range(2):
        s.w_own[layer] = s.weights[:, layer, :]
    s.head_own[...] = jnp.zeros_like(s.head_own)
    s.head_own[:, 0 : s.V] = s.head[...]
    s.cut_input(0)
    greet(chips, members)
    lw1.start()
    gx[0].start()
    for m in range(1, H):
        s.cut_input(m)
    s.pad[...] = jnp.zeros_like(s.pad)
    lw1.wait()
    gw1.start()
    for g in later:
        g.start()
    s.tables()
    s.turn_inputs()
    gx[0].relay_first()
    gw1.relay_first()
    for g in later:
        g.relay_first()
    gx[0].relay_rest()
    gw1.relay_rest()
    for m in range(1, H):
        gx[m].start()
    gw1.finish()
    settle()

    last = H * PU - 1

    def ready_x(m):
        gx[m].finish()
        s.rims_from(s.edges_x[m], m)

    def send_a(m):
        s.cut_act(m)
        ga[m].start()

    def ready_a(m):
        ga[m].finish()
        s.rims_from(s.edges_a[m], m)

    before = {m * PU: functools.partial(ready_x, m) for m in range(H)}
    after = []
    for m in range(1, H):
        at = m * PU - 1
        after.append((at, functools.partial(send_a, m - 1)))
        after.append((at, gx[m].relay_first))
        after.append((at, gx[m].relay_rest))
        after.append((min(at + 2, last), ga[m - 1].relay_first))
    hooked(H * PU, s.conv_first, before, merge(*after))
    s.cut_act(H - 1)
    ga[H - 1].start()
    for m in range(H - 1):
        ga[m].relay_rest()
    for g in later:
        g.relay_rest()
    for g in later:
        g.finish()
    settle_last()
    s.head_t[...] = s.heads[...].astype(f32).T.astype(bf16)

    before = {m * PU: functools.partial(ready_a, m) for m in range(H)}
    after = [
        (max((H - 1) * PU - 2, 0), ga[H - 1].relay_first),
        (max((H - 1) * PU - 1, 0), ga[H - 1].relay_rest),
    ]
    hooked(H * PU, s.conv_last, before, merge(*after))
    s.prepare_back()

    lax.fori_loop(0, PU, lambda p, carry: (s.score(p), carry)[1], 0)
    after = []
    late = []
    total = H * PU
    for p in range(PU):
        at = (p + 1) * H - 1
        after.append((at, gb[p].start))
        for step, todo in ((at + 2, gb[p].relay_first), (at + 4, gb[p].relay_rest)):
            if step < total:
                after.append((step, todo))
            else:
                late.append((min(step - total, s.n // s.K - 1), todo))
    hooked(total, s.backward, None, merge(*after))

    s.acc[...] = jnp.zeros_like(s.acc)
    hooked(s.n // s.K, lambda kb: s.products(kb, s.x3_two, slice(0, s.c)), None, merge(*late))
    s_two = Scatter(s.two, chips, members, [getattr(s, f"t{i}") for i in range(10)], s.csem.at[0])
    s_head = Scatter(s.hg_t, chips, members, [getattr(s, f"h{i}") for i in range(6)], s.csem.at[1])
    s_one = [
        Scatter(
            getattr(s, f"one{q}"),
            chips,
            members,
            [getattr(s, f"o{q}{i}") for i in range(10)],
            s.csem.at[2 + q],
        )
        for q in range(s.cuts)
    ]
    s.turn_out(s.two, slice(0, s.c))
    s.acc[...] = jnp.zeros_like(s.acc)
    put_rows(s.hg_t, 0, s.hg[...].T)
    s_two.core_start()
    s_head.core_start()

    for p in range(PU):
        gb[p].finish()
    for m in range(H):
        s.rims_back(m)
    s_two.core_done()
    s_head.core_done()
    lax.fori_loop(0, s.n, lambda k, carry: (s.slope_first(k), carry)[1], 0)
    wide = s.c // s.cuts
    cols = [slice(q * wide, (q + 1) * wide) for q in range(s.cuts)]
    for q in range(s.cuts):
        after = {0: s_one[q - 1].core_done} if q else None
        body = functools.partial(lambda at, kb: s.products(kb, s.x3_one, at), cols[q])
        hooked(s.n // s.K, body, None, after)
        s.turn_out(getattr(s, f"one{q}"), cols[q])
        s_one[q].core_start()
    s_two.chip_done()
    s_head.chip_done()
    s_one[-1].core_done()
    for q in range(s.cuts - 1):
        s_one[q].chip_done()
    s.grads[:, 1, :] = s_two.line_done()
    s.head_out[...] = s_head.line_done()
    s_one[-1].chip_done()
    for q in range(s.cuts):
        s.grads[:, 0, cols[q]] = s_one[q].line_done()
    for scatter in [s_two, s_head] + s_one:
        scatter.finish()
    for u in range(H * PU):
        for j in range(1, members):
            s.go(u, j).wait_send()
            s.home(u, j).wait_send()


def shards(faces, zs, features, observed, conv_weights, head_weight, adjacency, placement_map):
    H, T, h, w, c = features.shape
    n = H * T
    V = head_weight.shape[1]
    rows, hrows = conv_weights.shape[0], head_weight.shape[0]
    lanes = -(-V // 128) * 128
    chips = faces // 2
    G = 2 if T % 2 == 0 else 1
    PU = T // G
    K = 4 if n % 4 == 0 else (2 if n % 2 == 0 else 1)
    part = observed.shape[-1]
    cells = h * w
    cuts = 2 if c % 256 == 0 else 1
    dims = dict(
        H=H, T=T, h=h, w=w, c=c, n=n, V=V, rows=rows, hrows=hrows, chips=chips, Z=zs, G=G, P=PU,
        K=K, part=part, cuts=cuts,
    )
    side = 4 * w
    total_rows = rows * faces * zs
    total_heads = hrows * faces * zs
    scratch = {
        "at_face": SMEM((T * 4,), jnp.int32),
        "at_slot": SMEM((T * 4,), jnp.int32),
        "at_side": SMEM((T * 4,), jnp.int32),
        "turn": VMEM((T, side, side), bf16),
        "obs_wide": VMEM((PU, V, G * part), f32),
        "w_own": VMEM((2, rows, c), bf16),
        "rims": VMEM((n, side, c), f32),
        "field": VMEM((h, w, c), f32),
        "pad": VMEM((h + 2, w + 16, c), f32),
        "pad2": VMEM((h + 4, w + 16, c), f32),
        "head_own": VMEM((hrows, lanes), bf16),
        "w1": VMEM((total_rows, c), bf16),
        "w2": VMEM((total_rows, c), bf16),
        "heads": VMEM((total_heads, lanes), bf16),
        "head_t": VMEM((lanes, total_heads), bf16),
        "x3_one": VMEM((n, h + 2, w, 3 * c), bf16),
        "x3_two": VMEM((n, h + 2, w, 3 * c), bf16),
        "d_one": VMEM((n, cells, c), f32),
        "d_two": VMEM((n, cells, c), f32),
        "act_one": VMEM((n, cells, c), bf16),
        "act_two": VMEM((n, cells, c), bf16),
        "packed": VMEM((H * PU, zs, V, G * part), bf16),
        "came": VMEM((H * PU, zs, V, G * part), bf16),
        "slopes": VMEM((H * PU, zs, V, G * part), bf16),
        "back": VMEM((H * PU, zs, V, G * part), bf16),
        "va": VMEM((3, c, 3 * c), bf16),
        "vb": VMEM((2, c, 3 * c), bf16),
        "s3": VMEM((G, h + 4, w, 3 * c), bf16),
        "cols": VMEM((2, G, h, 3 * c), bf16),
        "inner": VMEM((n, h, w, c), bf16),
        "turned": VMEM((c, n * cells), bf16),
        "acc": VMEM((3, c, 3 * c), f32),
        "hg": VMEM((lanes, c), f32),
        "hg_t": VMEM((faces * zs, hrows, lanes), f32),
        "two": VMEM((faces * zs, rows, c), f32),
        "borders": VMEM((faces, PU * H * G * 4, w, c), bf16),
    }
    for m in range(H):
        scratch[f"edges_x{m}"] = VMEM((faces, T * 4, w, c), bf16)
        scratch[f"edges_a{m}"] = VMEM((faces, T * 4, w, c), bf16)
    sums = [("t", rows, c, True), ("h", hrows, lanes, False)]
    for q in range(cuts):
        scratch[f"one{q}"] = VMEM((faces * zs, rows, c // cuts), f32)
        sums.append((f"o{q}", rows, c // cuts, True))
    for name, r, lane, code in sums:
        for i, v in enumerate(scatter_scratch(chips, zs, r, lane, code)):
            scratch[f"{name}{i}"] = v
    scratch["w2_apart"] = VMEM((faces * zs, rows, c), bf16)
    scratch["heads_apart"] = VMEM((faces * zs, hrows, lanes), bf16)
    if rows % 16:
        scratch["w1_apart"] = VMEM((faces * zs, rows, c), bf16)
    dma = pltpu.SemaphoreType.DMA
    scratch["gsem"] = dma((3 + 2 * H + PU, 4, chips + 3))
    scratch["lsem"] = dma((1, 2, zs))
    scratch["psem"] = dma((2, 6, max(chips, zs)))
    scratch["ssem"] = dma((4, H * PU, zs))
    scratch["csem"] = dma((2 + cuts, 10, max(chips, zs)))
    vmem = pl.BlockSpec(memory_space=VMEM)
    smem = pl.BlockSpec(memory_space=SMEM)
    ins = ["place", "glue", "x", "obs", "weights", "head"]
    outs = ["grads", "head_out"]
    grads, head_out = pl.pallas_call(
        functools.partial(step_kernel, dims, ins + outs + list(scratch)),
        out_shape=[
            jax.ShapeDtypeStruct((rows, 2, c), f32),
            jax.ShapeDtypeStruct((hrows, lanes), f32),
        ],
        in_specs=[smem, smem] + [vmem] * 4,
        out_specs=[vmem] * 2,
        scratch_shapes=list(scratch.values()),
        compiler_params=pltpu.CompilerParams(
            collective_id=1, has_side_effects=True, vmem_limit_bytes=LIMIT
        ),
        name="step",
    )(
        placement_map,
        adjacency.transpose(2, 1, 0),
        features.reshape(n, cells, c),
        observed.transpose(0, 2, 1),
        conv_weights,
        head_weight,
    )
    return grads, head_out[:, :V]


def solution(mesh):
    in_specs = (
        P("member", "face", None, None, None),
        P("face", None, "member"),
        P(("face", "member"), None, None),
        P(("face", "member"), None),
        P(),
        P(),
    )
    out_specs = (P(("face", "member"), None, None), P(("face", "member"), None))
    body = functools.partial(shards, mesh.shape["face"], mesh.shape["member"])
    return jax.shard_map(body, mesh=mesh, in_specs=in_specs, out_specs=out_specs, check_vma=False)
```

```python
import functools

import jax
import jax.numpy as jnp
from jax import lax
from jax.experimental import pallas as pl
from jax.experimental.pallas import tpu as pltpu
from jax.sharding import PartitionSpec as P

smooth_sq = 0.0625
MESH = pl.DeviceIdType.MESH
VMEM = pltpu.VMEM
SMEM = pltpu.SMEM
f32 = jnp.float32
bf16 = jnp.bfloat16
i16 = jnp.int16
LIMIT = 62 * 1024 * 1024
TOP = 32767.0
NT = (((1,), (1,)), ((), ()))
TN = (((0,), (0,)), ((), ()))
NN = (((1,), (0,)), ((), ()))


def mm(a, b, dims=NN):
    return lax.dot_general(a, b, dims, preferred_element_type=f32)


def rcopy(src, dst, send, recv, **where):
    return pltpu.make_async_remote_copy(
        src_ref=src, dst_ref=dst, send_sem=send, recv_sem=recv, device_id=where, device_id_type=MESH
    )


def greet(chips, members):
    face = lax.axis_index("face")
    member = lax.axis_index("member")
    core = face % 2
    chip = face // 2
    barrier = pltpu.get_barrier_semaphore()
    pl.semaphore_signal(
        barrier, inc=1, device_id={"face": chip * 2 + 1 - core}, device_id_type=MESH
    )
    for j in range(1, chips):
        pl.semaphore_signal(
            barrier,
            inc=1,
            device_id={"face": ((chip + j) % chips) * 2 + core},
            device_id_type=MESH,
        )
    for j in range(1, members):
        pl.semaphore_signal(
            barrier, inc=1, device_id={"member": (member + j) % members}, device_id_type=MESH
        )
    return lambda: pl.semaphore_wait(barrier, chips + members - 1)


class FaceGather:
    def __init__(self, at, chips, sems):
        self.at, self.chips, self.sems = at, chips, sems
        face = lax.axis_index("face")
        self.face, self.core, self.chip = face, face % 2, face // 2
        self.partner = self.chip * 2 + 1 - self.core

    def direct(self, j):
        mine = self.at(self.face, None)
        return rcopy(
            mine,
            mine,
            self.sems.at[0, j],
            self.sems.at[1, j],
            face=((self.chip + j) % self.chips) * 2 + self.core,
        )

    def forward(self, j):
        block = self.at(((self.chip + self.chips - j) % self.chips) * 2 + self.core, None)
        return rcopy(block, block, self.sems.at[2, j], self.sems.at[3, j], face=self.partner)

    def start(self):
        for j in range(1, self.chips):
            self.direct(j).start()
        self.forward(0).start()

    def relay_first(self):
        pass

    def relay_rest(self):
        for j in range(1, self.chips):
            self.direct(j).wait_recv()
            self.forward(j).start()

    def finish(self):
        for j in range(1, self.chips):
            self.direct(j).wait_send()
        for j in range(self.chips):
            self.forward(j).wait()


class SquareGather:
    def __init__(self, at, chips, sems):
        self.at, self.sems = at, sems
        face = lax.axis_index("face")
        core, chip = face % 2, face // 2
        col, row = chip % 2, chip // 2
        self.face = face
        self.partner = chip * 2 + 1 - core
        self.beside = (row * 2 + 1 - col) * 2 + core
        self.below = ((1 - row) * 2 + col) * 2 + core
        self.across = ((1 - row) * 2 + 1 - col) * 2 + core

    def direct(self, k):
        to = (self.beside, self.beside, self.below, self.below, self.below, self.beside)[k]
        block = (self.face,) * 4 + (self.beside, self.below)
        ref = self.at(block[k], (0, 1, 1, 0, 0, 1)[k])
        return rcopy(ref, ref, self.sems.at[0, k], self.sems.at[1, k], face=to)

    def forward(self, k):
        if k == 6:
            ref = self.at(self.face, None)
        else:
            block = (
                self.beside,
                self.beside,
                self.below,
                self.below,
                self.across,
                self.across,
            )
            ref = self.at(block[k], (0, 1, 1, 0, 0, 1)[k])
        return rcopy(ref, ref, self.sems.at[2, k], self.sems.at[3, k], face=self.partner)

    def start(self):
        for k in (0, 2, 1, 3):
            self.direct(k).start()
        self.forward(6).start()

    def relay_first(self):
        for k, onward in ((0, 4), (2, 5)):
            self.direct(k).wait_recv()
            self.direct(onward).start()
            self.forward(k).start()

    def relay_rest(self):
        for k in (1, 3, 4, 5):
            self.direct(k).wait_recv()
            self.forward(k).start()

    def finish(self):
        for k in range(6):
            self.direct(k).wait_send()
        for k in range(7):
            self.forward(k).wait()


def units(ref, rows, start, count):
    if len(ref.shape) == 3:
        return ref.at[pl.ds(start, count)] if count > 1 else ref.at[start]
    return ref.at[pl.ds(pl.multiple_of(start * rows, rows), count * rows)]


def gather_rows(ref, rows, members, chips, sems):
    def at(block, part):
        if part is None:
            return units(ref, rows, block * members, members)
        half = members // 2
        return units(ref, rows, block * members + part * half, half)

    return (SquareGather if chips == 4 and members % 2 == 0 else FaceGather)(at, chips, sems)


def gather_edges(ref, start, count, chips, sems):
    def at(block, part):
        if part is None:
            return ref.at[block, pl.ds(start, count)]
        half = count // 2
        return ref.at[block, pl.ds(start + part * half, half)]

    return (SquareGather if chips == 4 and count % 2 == 0 else FaceGather)(at, chips, sems)


class LineGather:
    def __init__(self, src, ref, rows, members, sems):
        self.src, self.ref, self.rows, self.members, self.sems = src, ref, rows, members, sems
        self.face, self.member = lax.axis_index("face"), lax.axis_index("member")

    def at(self, member):
        return units(self.ref, self.rows, self.face * self.members + member, 1)

    def own(self):
        return pltpu.make_async_copy(self.src, self.at(self.member), self.sems.at[0, 0])

    def send(self, j):
        to = (self.member + j) % self.members
        return rcopy(
            self.src, self.at(self.member), self.sems.at[0, j], self.sems.at[1, j], member=to
        )

    def came(self, j):
        origin = (self.member + self.members - j) % self.members
        return rcopy(
            self.src, self.at(origin), self.sems.at[0, j], self.sems.at[1, j], member=origin
        )

    def start(self):
        self.own().start()
        for j in range(1, self.members):
            self.send(j).start()

    def wait(self):
        self.own().wait()
        for j in range(1, self.members):
            self.came(j).wait_recv()
            self.send(j).wait_send()


class PlaneLine:
    def __init__(self, src, ref, chips, members, sems):
        self.src, self.ref, self.chips, self.members, self.sems = src, ref, chips, members, sems
        self.member = lax.axis_index("member")
        face = lax.axis_index("face")
        self.core, self.chip = face % 2, face // 2
        self.partner = self.chip * 2 + 1 - self.core

    def mine(self):
        return self.ref.at[(self.member * 2 + self.core) * self.chips + self.chip]

    def own(self):
        return pltpu.make_async_copy(self.src, self.mine(), self.sems.at[0, 0])

    def plane(self, j):
        to = ((self.chip + j) % self.chips) * 2 + self.core
        return rcopy(self.src, self.mine(), self.sems.at[0, j], self.sems.at[1, j], face=to)

    def group(self, j):
        member = (self.member + self.members - j) % self.members
        return self.ref.at[pl.ds((member * 2 + self.core) * self.chips, self.chips)]

    def line(self, j):
        to = (self.member + j) % self.members
        ref = self.group(0)
        return rcopy(ref, ref, self.sems.at[2, j], self.sems.at[3, j], member=to)

    def cross(self, j):
        ref = self.group(j)
        return rcopy(ref, ref, self.sems.at[4, j], self.sems.at[5, j], face=self.partner)

    def start(self):
        self.own().start()
        for j in range(1, self.chips):
            self.plane(j).start()

    def relay_first(self):
        self.own().wait()
        for j in range(1, self.chips):
            self.plane(j).wait_recv()
        for j in range(1, self.members):
            self.line(j).start()
        self.cross(0).start()

    def relay_rest(self):
        for j in range(1, self.members):
            self.line(j).wait_recv()
            self.cross(j).start()

    def finish(self):
        for j in range(1, self.chips):
            self.plane(j).wait_send()
        for j in range(1, self.members):
            self.line(j).wait_send()
        for j in range(self.members):
            self.cross(j).wait()


def coded(v):
    axes = tuple(range(v.ndim - 1))
    most = jnp.max(jnp.abs(v), axis=axes, keepdims=True)
    code = jnp.round(v * (TOP / jnp.maximum(most, 1e-33))).astype(jnp.int32).astype(i16)
    most = most.reshape(1, v.shape[-1])
    return code, jnp.broadcast_to(most * (1.0 / TOP), (8, v.shape[-1]))


def decoded(code, scale):
    return code.astype(jnp.int32).astype(f32) * scale[0:1, :]


class Scatter:
    def __init__(self, g, chips, members, scratch, sems):
        self.g, self.chips, self.members = g, chips, members
        self.fromcore, self.acc, self.out1, self.in1, self.out2, self.in2 = scratch[:6]
        self.sc = scratch[6:]
        self.sems = sems
        face = lax.axis_index("face")
        self.member = lax.axis_index("member")
        self.core, self.chip = face % 2, face // 2
        self.partner = self.chip * 2 + 1 - self.core
        self.order = list(range(1, chips)) + [0]

    def part(self, chip, core):
        return pl.ds((chip * 2 + core) * self.members, self.members)

    def there(self, j):
        return (self.chip + j) % self.chips

    def core_copy(self, j):
        return rcopy(
            self.g.at[self.part(self.there(j), 1 - self.core)],
            self.fromcore.at[j],
            self.sems.at[0, j],
            self.sems.at[1, j],
            face=self.partner,
        )

    def copies(self, first, boxes, j, **to):
        s = self.sems
        return [
            rcopy(a.at[j], b.at[j], s.at[i, j], s.at[i + 1, j], **to)
            for i, (a, b) in zip((first, first + 2), boxes)
        ]

    def chip_copies(self, j):
        boxes = [(self.out1, self.in1)] + ([(self.sc[0], self.sc[1])] if self.sc else [])
        return self.copies(2, boxes, j, face=self.there(j) * 2 + self.core)

    def line_copies(self, j):
        boxes = [(self.out2, self.in2)] + ([(self.sc[2], self.sc[3])] if self.sc else [])
        return self.copies(6, boxes, j, member=(self.member + j) % self.members)

    def core_start(self):
        for j in self.order:
            self.core_copy(j).start()

    def core_done(self):
        for j in self.order:
            self.core_copy(j).wait_recv()
            total = self.g[self.part(self.there(j), self.core)] + self.fromcore[j]
            if j == 0:
                self.acc[...] = total
                continue
            if self.sc:
                self.out1[j], self.sc[0][j] = coded(total)
            else:
                self.out1[j] = total
            for c in self.chip_copies(j):
                c.start()

    def summed(self, to):
        v = self.acc[to]
        for i in range(1, self.chips):
            piece = self.in1[i, to]
            v = v + (decoded(piece, self.sc[1][i]) if self.sc else piece)
        return v

    def chip_done(self):
        for j in range(1, self.chips):
            for c in self.chip_copies(j):
                c.wait_recv()
        for j in range(1, self.members):
            v = self.summed((self.member + j) % self.members)
            if self.sc:
                self.out2[j], self.sc[2][j] = coded(v)
            else:
                self.out2[j] = v
            for c in self.line_copies(j):
                c.start()

    def line_done(self):
        total = self.summed(self.member)
        for j in range(1, self.members):
            for c in self.line_copies(j):
                c.wait_recv()
            piece = self.in2[j]
            total = total + (decoded(piece, self.sc[3][j]) if self.sc else piece)
        return total

    def finish(self):
        for j in range(self.chips):
            self.core_copy(j).wait_send()
        for j in range(1, self.chips):
            for c in self.chip_copies(j):
                c.wait_send()
        for j in range(1, self.members):
            for c in self.line_copies(j):
                c.wait_send()


def scatter_scratch(chips, members, rows, lanes, code):
    kind = i16 if code else f32
    out = [
        VMEM((chips, members, rows, lanes), f32),
        VMEM((members, rows, lanes), f32),
        VMEM((chips, members, rows, lanes), kind),
        VMEM((chips, members, rows, lanes), kind),
        VMEM((members, rows, lanes), kind),
        VMEM((members, rows, lanes), kind),
    ]
    if code:
        out += [VMEM((chips, 8, lanes), f32)] * 2 + [VMEM((members, 8, lanes), f32)] * 2
    return out


def put_rows(ref, first, v):
    rows, done = ref.shape[1], 0
    while done < v.shape[0]:
        block, at = divmod(first + done, rows)
        size = min(rows - at, v.shape[0] - done)
        ref[block, at : at + size, :] = v[done : done + size]
        done += size


def sides_of(field):
    h, w, c = field.shape
    return [
        field[0],
        field[:, w - 1 : w, :].reshape(h, c),
        field[h - 1],
        field[:, 0:1, :].reshape(h, c),
    ]


def g_of(v):
    return v * lax.rsqrt(v * v + smooth_sq)


class Step:
    def __init__(self, dims, refs):
        self.__dict__.update(dims)
        self.__dict__.update(refs)
        face = lax.axis_index("face")
        self.face, self.member = face, lax.axis_index("member")


    def tables(self):
        first = self.face * self.T
        total = self.place.shape[0]

        def fill(i, carry):
            tile = self.place[first + i]
            for a in range(4):
                want = self.glue[0, a, tile]

                def look(s, slot):
                    return jnp.where(self.place[s] == want, s, slot)

                slot = lax.fori_loop(0, total, look, jnp.int32(0), unroll=8)
                owner = slot // self.T
                self.at_face[i * 4 + a] = owner
                self.at_slot[i * 4 + a] = slot - owner * self.T
                self.at_side[i * 4 + a] = self.glue[1, a, tile]
            size = 4 * self.w
            row = lax.broadcasted_iota(jnp.int32, (size, size), 0)
            col = lax.broadcasted_iota(jnp.int32, (size, size), 1)
            side = row // self.w
            at = row - side * self.w
            flag = jnp.zeros((size, size), jnp.int32)
            for a in range(4):
                flag = jnp.where(side == a, self.glue[2, a, tile], flag)
            target = side * self.w + jnp.where(flag == 1, self.w - 1 - at, at)
            self.turn[i] = jnp.where(col == target, 1.0, 0.0).astype(bf16)
            return carry

        lax.fori_loop(0, self.T, fill, 0)

    def rims_from(self, box, m):
        def one(i, carry):
            cat = jnp.concatenate(
                [
                    box[self.at_face[i * 4 + a], self.at_slot[i * 4 + a] * 4 + self.at_side[i * 4 + a]]
                    for a in range(4)
                ],
                axis=0,
            )
            self.rims[m * self.T + i] = mm(self.turn[i], cat)
            return carry

        lax.fori_loop(0, self.T, one, 0, unroll=True)

    def turn_inputs(self):
        for p in range(self.P):
            o = [self.obs[p * self.G + g].astype(f32).T for g in range(self.G)]
            self.obs_wide[p] = jnp.concatenate(o, axis=1) if self.G > 1 else o[0]

    def cut(self, box, i):
        for a, v in enumerate(sides_of(self.field)):
            box[self.face, i * 4 + a] = v.astype(bf16)

    def cut_input(self, m):
        def one(i, carry):
            v = self.x[m * self.T + i].astype(f32)
            self.field[...] = v.reshape(self.h, self.w, self.c)
            self.cut(self.edges_x[m], i)
            return carry

        lax.fori_loop(0, self.T, one, 0)


    def conv(self, u, src, x3, w_ref, slope):
        h, w, c, G = self.h, self.w, self.c, self.G
        k0 = u * G
        pad = self.pad
        for g in range(G):
            k = k0 + g
            rims = self.rims[k]
            pad[1 : h + 1, 8 : 8 + w, :] = src[k].reshape(h, w, c).astype(f32)
            pad[0, 8 : 8 + w, :] = rims[0:w]
            pad[1 : h + 1, 8 + w : 9 + w, :] = rims[w : w + h].reshape(h, 1, c)
            pad[h + 1, 8 : 8 + w, :] = rims[w + h : 2 * w + h]
            pad[1 : h + 1, 7:8, :] = rims[2 * w + h :].reshape(h, 1, c)
            for b in range(3):
                x3[k, :, :, b * c : (b + 1) * c] = pad[:, 7 + b : 7 + b + w, :].astype(bf16)
        pre = None
        for a in range(3):
            part = mm(
                x3[pl.ds(k0, G), a : a + h].reshape(G * h * w, 3 * c),
                w_ref[3 * a * c : 3 * (a + 1) * c, :],
            )
            pre = part if pre is None else pre + part
        s = 1.0 / (1.0 + jnp.exp(-pre))
        act = pre * s
        slope[pl.ds(k0, G)] = (s + act * (1.0 - s)).reshape(G, h * w, c)
        return act.astype(bf16)

    def conv_first(self, u):
        act = self.conv(u, self.x, self.x3_one, self.w1, self.d_one)
        cells = self.h * self.w
        for g in range(self.G):
            self.act_one[u * self.G + g] = act[g * cells : (g + 1) * cells]

    def cut_act(self, m):
        h, w, c = self.h, self.w, self.c

        def one(i, carry):
            self.field[...] = self.act_one[m * self.T + i].astype(f32).reshape(h, w, c)
            self.cut(self.edges_a[m], i)
            return carry

        lax.fori_loop(0, self.T, one, 0)

    def go(self, u, j):
        to = (self.member + j) % self.Z
        return rcopy(
            self.packed.at[u, to],
            self.came.at[u, j],
            self.ssem.at[0, u, j],
            self.ssem.at[1, u, j],
            member=to,
        )

    def home(self, i, j, here=False):
        back = (self.member + j) % self.Z if here else self.member
        return rcopy(
            self.slopes.at[i, j],
            self.back.at[i, back],
            self.ssem.at[2, i, j],
            self.ssem.at[3, i, j],
            member=(self.member + self.Z - j) % self.Z,
        )

    def conv_last(self, u):
        act = self.conv(u, self.act_one, self.x3_two, self.w2, self.d_two)
        G, cells, part = self.G, self.h * self.w, self.part
        outs = []
        for g in range(G):
            own = act[g * cells : (g + 1) * cells]
            self.act_two[u * G + g] = own
            outs.append(mm(self.head_t[0 : self.V, :], own, NT).astype(bf16))
        for q in range(self.Z):
            cols = [o[:, q * part : (q + 1) * part] for o in outs]
            self.packed[u, q] = jnp.concatenate(cols, axis=1) if G > 1 else cols[0]
        for j in range(1, self.Z):
            self.go(u, j).start()


    def score(self, p):
        ensemble = self.H * self.Z
        for m in range(self.H):
            for j in range(1, self.Z):
                self.go(m * self.P + p, j).wait_recv()
        rows = 16 if self.V % 16 == 0 else self.V
        for r in range(0, self.V, rows):
            at = slice(r, r + rows)
            o = self.obs_wide[p, at, :]
            names = [(m, j) for j in range(self.Z) for m in range(self.H)]
            vals = []
            for m, j in names:
                u = m * self.P + p
                v = self.packed[u, self.member, at, :] if j == 0 else self.came[u, j, at, :]
                vals.append(v.astype(f32))
            paired = [None] * len(vals)
            for a in range(len(vals)):
                for b in range(a + 1, len(vals)):
                    t = g_of(vals[a] - vals[b])
                    paired[a] = t if paired[a] is None else paired[a] + t
                    paired[b] = -t if paired[b] is None else paired[b] - t
            for (m, j), v, t in zip(names, vals, paired):
                i = p * self.H + m
                s = (g_of(v - o) / ensemble - t / (ensemble * ensemble)) / self.h
                if j == 0:
                    self.back[i, self.member, at, :] = s.astype(bf16)
                else:
                    self.slopes[i, j, at, :] = s.astype(bf16)
        for m in range(self.H):
            for j in range(1, self.Z):
                self.home(p * self.H + m, j).start()


    def prepare_back(self):
        c = self.c
        for a in range(3):
            for b in range(3):
                tap = self.w2[(3 * a + b) * c : (3 * a + b + 1) * c, :]
                self.va[a, :, b * c : (b + 1) * c] = tap
                if b == 0:
                    self.vb[0, :, a * c : (a + 1) * c] = tap
                if b == 2:
                    self.vb[1, :, a * c : (a + 1) * c] = tap
        self.hg[...] = jnp.zeros_like(self.hg)
        self.pad2[...] = jnp.zeros_like(self.pad2)

    def lanes(self, k):
        cells = self.h * self.w
        return pl.ds(pl.multiple_of(k * cells, cells), cells)

    def backward(self, i):
        h, w, c, G, H, part = self.h, self.w, self.c, self.G, self.H, self.part
        p = i // H
        m = i - p * H
        u = m * self.P + p
        for j in range(1, self.Z):
            self.home(i, j, here=True).wait_recv()
        pad = self.pad2
        for g in range(G):
            k = u * G + g
            slope_out = jnp.concatenate(
                [self.back[i, q][:, g * part : (g + 1) * part] for q in range(self.Z)], axis=1
            )
            self.hg[0 : self.V, :] += mm(slope_out, self.act_two[k])
            back = mm(slope_out, self.head_t[0 : self.V, :], TN)
            slope = (back * self.d_two[k]).astype(bf16)
            self.turned[:, self.lanes(k)] = slope.T
            pad[2 : h + 2, 8 : 8 + w, :] = slope.astype(f32).reshape(h, w, c)
            for b in range(3):
                self.s3[g, :, :, b * c : (b + 1) * c] = pad[:, 9 - b : 9 - b + w, :].astype(bf16)
            left = pad[:, 8:9, :].reshape(h + 4, c)
            right = pad[:, 7 + w : 8 + w, :].reshape(h + 4, c)
            for a in range(3):
                self.cols[0, g, :, a * c : (a + 1) * c] = left[3 - a : 3 - a + h].astype(bf16)
                self.cols[1, g, :, a * c : (a + 1) * c] = right[3 - a : 3 - a + h].astype(bf16)
        full = None
        for a in range(3):
            lhs = self.s3[:, 2 - a : 4 - a + h].reshape(G * (h + 2) * w, 3 * c)
            one = mm(lhs, self.va[a], NT)
            full = one if full is None else full + one
        full = full.reshape(G, h + 2, w, c).astype(bf16)
        self.inner[pl.ds(u * G, G)] = full[:, 1 : h + 1]
        lefts = mm(self.cols[0].reshape(G * h, 3 * c), self.vb[0], NT).astype(bf16)
        rights = mm(self.cols[1].reshape(G * h, 3 * c), self.vb[1], NT).astype(bf16)
        for g in range(G):
            at = (i * G + g) * 4
            sides = (
                full[g, 0],
                rights[g * h : (g + 1) * h],
                full[g, h + 1],
                lefts[g * h : (g + 1) * h],
            )
            for a in range(4):
                self.borders[self.face, at + a] = sides[a]

    def rims_back(self, m):
        G = self.G

        def one(i, carry):
            sides = []
            for a in range(4):
                at = i * 4 + a
                slot = self.at_slot[at]
                unit = slot // G
                j = (m * G + slot - unit * G) * 4 + self.at_side[at]
                sides.append(self.borders[self.at_face[at], unit * (self.H * G * 4) + j])
            self.rims[m * self.T + i] = mm(self.turn[i], jnp.concatenate(sides, axis=0))
            return carry

        lax.fori_loop(0, self.T, one, 0, unroll=True)

    def slope_first(self, k):
        h, w, c = self.h, self.w, self.c
        rims, field = self.rims[k], self.field
        field[...] = self.inner[k].astype(f32)
        field[0] += rims[0:w]
        field[:, w - 1 : w, :] += rims[w : w + h].reshape(h, 1, c)
        field[h - 1] += rims[w + h : 2 * w + h]
        field[:, 0:1, :] += rims[2 * w + h :].reshape(h, 1, c)
        slope = (field[...].reshape(h * w, c) * self.d_one[k]).astype(bf16)
        self.turned[:, self.lanes(k)] = slope.T

    def products(self, kb, x3, cols):
        h, w, c, K = self.h, self.w, self.c, self.K
        cells = h * w
        at = pl.ds(pl.multiple_of(kb * K * cells, K * cells), K * cells)
        for a in range(3):
            rhs = x3[pl.ds(kb * K, K), a : a + h].reshape(K * cells, 3 * c)
            self.acc[a, cols, :] += mm(self.turned[cols, at], rhs)

    def turn_out(self, ref, cols):
        c = self.c
        for a in range(3):
            for b in range(3):
                put_rows(ref, (3 * a + b) * c, self.acc[a, cols, b * c : (b + 1) * c].T)


def hooked(steps, body, before=None, after=None):
    before, after = before or {}, after or {}

    def one(i, carry):
        for s, todo in sorted(before.items()):
            pl.when(i == s)(todo)
        body(i)
        for s, todo in sorted(after.items()):
            pl.when(i == s)(todo)
        return carry

    lax.fori_loop(0, steps, one, 0)


def merge(*items):
    out = {}
    for at, todo in items:
        out.setdefault(at, []).append(todo)

    def run(todos):
        def go():
            for t in todos:
                t()

        return go

    return {at: run(todos) for at, todos in out.items()}


def step_kernel(dims, names, *refs):
    s = Step(dims, dict(zip(names, refs)))
    chips, members, H, PU = s.chips, s.Z, s.H, s.P
    gsem = s.gsem
    s.edges_x = [getattr(s, f"edges_x{m}") for m in range(H)]
    s.edges_a = [getattr(s, f"edges_a{m}") for m in range(H)]
    w1 = s.w1_apart if hasattr(s, "w1_apart") else s.w1

    def settle():
        if hasattr(s, "w1_apart"):
            for d in range(chips * 2 * members):
                s.w1[d * s.rows : (d + 1) * s.rows, :] = s.w1_apart[d]

    def settle_last():
        for d in range(chips * 2 * members):
            face, member = divmod(d, members)
            at = (member * 2 + face % 2) * chips + face // 2
            s.w2[d * s.rows : (d + 1) * s.rows, :] = s.w2_apart[at]
            s.heads[d * s.hrows : (d + 1) * s.hrows, :] = s.heads_apart[at]

    lw1 = LineGather(s.w_own.at[0], w1, s.rows, members, s.lsem.at[0])
    gw1 = gather_rows(w1, s.rows, members, chips, gsem.at[0])
    later = [
        PlaneLine(s.w_own.at[1], s.w2_apart, chips, members, s.psem.at[0]),
        PlaneLine(s.head_own, s.heads_apart, chips, members, s.psem.at[1]),
    ]
    sides, share = s.T * 4, H * s.G * 4
    gx = [gather_edges(s.edges_x[m], 0, sides, chips, gsem.at[3 + m]) for m in range(H)]
    ga = [gather_edges(s.edges_a[m], 0, sides, chips, gsem.at[3 + H + m]) for m in range(H)]
    gb = [
        gather_edges(s.borders, p * share, share, chips, gsem.at[3 + 2 * H + p])
        for p in range(PU)
    ]

    all_here = greet(chips, members)
    for layer in range(2):
        s.w_own[layer] = s.weights[:, layer, :]
    s.head_own[...] = jnp.zeros_like(s.head_own)
    s.head_own[:, 0 : s.V] = s.head[...]
    s.cut_input(0)
    all_here()
    lw1.start()
    gx[0].start()
    for m in range(1, H):
        s.cut_input(m)
    s.pad[...] = jnp.zeros_like(s.pad)
    lw1.wait()
    gw1.start()
    for g in later:
        g.start()
    s.tables()
    s.turn_inputs()
    gx[0].relay_first()
    gw1.relay_first()
    for g in later:
        g.relay_first()
    gx[0].relay_rest()
    gw1.relay_rest()
    for m in range(1, H):
        gx[m].start()
    gw1.finish()
    settle()

    last = H * PU - 1

    def ready_x(m):
        gx[m].finish()
        s.rims_from(s.edges_x[m], m)

    def send_a(m):
        s.cut_act(m)
        ga[m].start()

    def ready_a(m):
        ga[m].finish()
        s.rims_from(s.edges_a[m], m)

    before = {m * PU: functools.partial(ready_x, m) for m in range(H)}
    after = []
    for m in range(1, H):
        at = m * PU - 1
        after.append((at, functools.partial(send_a, m - 1)))
        after.append((at, gx[m].relay_first))
        after.append((at, gx[m].relay_rest))
        after.append((at, ga[m - 1].relay_first))
    hooked(H * PU, s.conv_first, before, merge(*after))
    s.cut_act(H - 1)
    ga[H - 1].start()
    for m in range(H - 1):
        ga[m].relay_rest()
    for g in later:
        g.relay_rest()
    for g in later:
        g.finish()
    settle_last()
    s.head_t[...] = s.heads[...].astype(f32).T.astype(bf16)

    before = {m * PU: functools.partial(ready_a, m) for m in range(H)}
    after = [
        (max((H - 1) * PU - 3, 0), ga[H - 1].relay_first),
        (max((H - 1) * PU - 1, 0), ga[H - 1].relay_rest),
    ]
    hooked(H * PU, s.conv_last, before, merge(*after))
    s.prepare_back()

    lax.fori_loop(0, PU, lambda p, carry: (s.score(p), carry)[1], 0)
    after = []
    late = []
    total = H * PU
    for p in range(PU):
        at = (p + 1) * H - 1
        after.append((at, gb[p].start))
        for step, todo in ((at + 2, gb[p].relay_first), (at + 4, gb[p].relay_rest)):
            if step < total:
                after.append((step, todo))
            else:
                late.append((min(step - total, s.n // s.K - 1), todo))
    hooked(total, s.backward, None, merge(*after))

    s.acc[...] = jnp.zeros_like(s.acc)
    hooked(s.n // s.K, lambda kb: s.products(kb, s.x3_two, slice(0, s.c)), None, merge(*late))
    s_two = Scatter(s.two, chips, members, [getattr(s, f"t{i}") for i in range(10)], s.csem.at[0])
    s_head = Scatter(s.hg_t, chips, members, [getattr(s, f"h{i}") for i in range(6)], s.csem.at[1])
    s_one = [
        Scatter(
            getattr(s, f"one{q}"),
            chips,
            members,
            [getattr(s, f"o{q}{i}") for i in range(10)],
            s.csem.at[2 + q],
        )
        for q in range(s.cuts)
    ]
    s.turn_out(s.two, slice(0, s.c))
    s.acc[...] = jnp.zeros_like(s.acc)
    put_rows(s.hg_t, 0, s.hg[...].T)
    s_two.core_start()
    s_head.core_start()

    for p in range(PU):
        gb[p].finish()
    for m in range(H):
        s.rims_back(m)
    s_two.core_done()
    s_head.core_done()
    lax.fori_loop(0, s.n, lambda k, carry: (s.slope_first(k), carry)[1], 0)
    wide = s.c // s.cuts
    cols = [slice(q * wide, (q + 1) * wide) for q in range(s.cuts)]
    for q in range(s.cuts):
        after = {0: s_one[q - 1].core_done} if q else None
        body = functools.partial(lambda at, kb: s.products(kb, s.x3_one, at), cols[q])
        hooked(s.n // s.K, body, None, after)
        s.turn_out(getattr(s, f"one{q}"), cols[q])
        s_one[q].core_start()
    s_two.chip_done()
    s_head.chip_done()
    s_one[-1].core_done()
    for q in range(s.cuts - 1):
        s_one[q].chip_done()
    s.grads[:, 1, :] = s_two.line_done()
    s.head_out[...] = s_head.line_done()
    s_one[-1].chip_done()
    for q in range(s.cuts):
        s.grads[:, 0, cols[q]] = s_one[q].line_done()
    for scatter in [s_two, s_head] + s_one:
        scatter.finish()
    for u in range(H * PU):
        for j in range(1, members):
            s.go(u, j).wait_send()
            s.home(u, j).wait_send()


def shards(faces, zs, features, observed, conv_weights, head_weight, adjacency, placement_map):
    H, T, h, w, c = features.shape
    n = H * T
    V = head_weight.shape[1]
    rows, hrows = conv_weights.shape[0], head_weight.shape[0]
    lanes = -(-V // 128) * 128
    chips = faces // 2
    G = 2 if T % 2 == 0 else 1
    PU = T // G
    K = 6 if n % 6 == 0 else (2 if n % 2 == 0 else 1)
    part = observed.shape[-1]
    cells = h * w
    cuts = 2 if c % 256 == 0 else 1
    dims = dict(
        H=H, T=T, h=h, w=w, c=c, n=n, V=V, rows=rows, hrows=hrows, chips=chips, Z=zs, G=G, P=PU,
        K=K, part=part, cuts=cuts,
    )
    side = 4 * w
    total_rows = rows * faces * zs
    total_heads = hrows * faces * zs
    scratch = {
        "at_face": SMEM((T * 4,), jnp.int32),
        "at_slot": SMEM((T * 4,), jnp.int32),
        "at_side": SMEM((T * 4,), jnp.int32),
        "turn": VMEM((T, side, side), bf16),
        "obs_wide": VMEM((PU, V, G * part), f32),
        "w_own": VMEM((2, rows, c), bf16),
        "rims": VMEM((n, side, c), f32),
        "field": VMEM((h, w, c), f32),
        "pad": VMEM((h + 2, w + 16, c), f32),
        "pad2": VMEM((h + 4, w + 16, c), f32),
        "head_own": VMEM((hrows, lanes), bf16),
        "w1": VMEM((total_rows, c), bf16),
        "w2": VMEM((total_rows, c), bf16),
        "heads": VMEM((total_heads, lanes), bf16),
        "head_t": VMEM((lanes, total_heads), bf16),
        "x3_one": VMEM((n, h + 2, w, 3 * c), bf16),
        "x3_two": VMEM((n, h + 2, w, 3 * c), bf16),
        "d_one": VMEM((n, cells, c), f32),
        "d_two": VMEM((n, cells, c), f32),
        "act_one": VMEM((n, cells, c), bf16),
        "act_two": VMEM((n, cells, c), bf16),
        "packed": VMEM((H * PU, zs, V, G * part), bf16),
        "came": VMEM((H * PU, zs, V, G * part), bf16),
        "slopes": VMEM((H * PU, zs, V, G * part), bf16),
        "back": VMEM((H * PU, zs, V, G * part), bf16),
        "va": VMEM((3, c, 3 * c), bf16),
        "vb": VMEM((2, c, 3 * c), bf16),
        "s3": VMEM((G, h + 4, w, 3 * c), bf16),
        "cols": VMEM((2, G, h, 3 * c), bf16),
        "inner": VMEM((n, h, w, c), bf16),
        "turned": VMEM((c, n * cells), bf16),
        "acc": VMEM((3, c, 3 * c), f32),
        "hg": VMEM((lanes, c), f32),
        "hg_t": VMEM((faces * zs, hrows, lanes), f32),
        "two": VMEM((faces * zs, rows, c), f32),
        "borders": VMEM((faces, PU * H * G * 4, w, c), bf16),
    }
    for m in range(H):
        scratch[f"edges_x{m}"] = VMEM((faces, T * 4, w, c), bf16)
        scratch[f"edges_a{m}"] = VMEM((faces, T * 4, w, c), bf16)
    sums = [("t", rows, c, True), ("h", hrows, lanes, False)]
    for q in range(cuts):
        scratch[f"one{q}"] = VMEM((faces * zs, rows, c // cuts), f32)
        sums.append((f"o{q}", rows, c // cuts, True))
    for name, r, lane, code in sums:
        for i, v in enumerate(scatter_scratch(chips, zs, r, lane, code)):
            scratch[f"{name}{i}"] = v
    scratch["w2_apart"] = VMEM((faces * zs, rows, c), bf16)
    scratch["heads_apart"] = VMEM((faces * zs, hrows, lanes), bf16)
    if rows % 16:
        scratch["w1_apart"] = VMEM((faces * zs, rows, c), bf16)
    dma = pltpu.SemaphoreType.DMA
    scratch["gsem"] = dma((3 + 2 * H + PU, 4, chips + 3))
    scratch["lsem"] = dma((1, 2, zs))
    scratch["psem"] = dma((2, 6, max(chips, zs)))
    scratch["ssem"] = dma((4, H * PU, zs))
    scratch["csem"] = dma((2 + cuts, 10, max(chips, zs)))
    vmem = pl.BlockSpec(memory_space=VMEM)
    smem = pl.BlockSpec(memory_space=SMEM)
    ins = ["place", "glue", "x", "obs", "weights", "head"]
    outs = ["grads", "head_out"]
    grads, head_out = pl.pallas_call(
        functools.partial(step_kernel, dims, ins + outs + list(scratch)),
        out_shape=[
            jax.ShapeDtypeStruct((rows, 2, c), f32),
            jax.ShapeDtypeStruct((hrows, lanes), f32),
        ],
        in_specs=[smem, smem] + [vmem] * 4,
        out_specs=[vmem] * 2,
        scratch_shapes=list(scratch.values()),
        compiler_params=pltpu.CompilerParams(
            collective_id=1, has_side_effects=True, vmem_limit_bytes=LIMIT
        ),
        name="step",
    )(
        placement_map,
        adjacency.transpose(2, 1, 0),
        features.reshape(n, cells, c),
        observed.transpose(0, 2, 1),
        conv_weights,
        head_weight,
    )
    return grads, head_out[:, :V]


def solution(mesh):
    in_specs = (
        P("member", "face", None, None, None),
        P("face", None, "member"),
        P(("face", "member"), None, None),
        P(("face", "member"), None),
        P(),
        P(),
    )
    out_specs = (P(("face", "member"), None, None), P(("face", "member"), None))
    body = functools.partial(shards, mesh.shape["face"], mesh.shape["member"])
    return jax.shard_map(body, mesh=mesh, in_specs=in_specs, out_specs=out_specs, check_vma=False)
```

```python
import functools

import jax
import jax.numpy as jnp
from jax import lax
from jax.experimental import pallas as pl
from jax.experimental.pallas import tpu as pltpu
from jax.sharding import PartitionSpec as P

smooth_sq = 0.0625
MESH = pl.DeviceIdType.MESH
VMEM = pltpu.VMEM
SMEM = pltpu.SMEM
f32 = jnp.float32
bf16 = jnp.bfloat16
i16 = jnp.int16
LIMIT = 62 * 1024 * 1024
TOP = 32767.0
NT = (((1,), (1,)), ((), ()))
TN = (((0,), (0,)), ((), ()))
NN = (((1,), (0,)), ((), ()))


def mm(a, b, dims=NN):
    return lax.dot_general(a, b, dims, preferred_element_type=f32)


def rcopy(src, dst, send, recv, **where):
    return pltpu.make_async_remote_copy(
        src_ref=src, dst_ref=dst, send_sem=send, recv_sem=recv, device_id=where, device_id_type=MESH
    )


def greet(chips, members):
    face = lax.axis_index("face")
    member = lax.axis_index("member")
    core = face % 2
    chip = face // 2
    barrier = pltpu.get_barrier_semaphore()
    pl.semaphore_signal(
        barrier, inc=1, device_id={"face": chip * 2 + 1 - core}, device_id_type=MESH
    )
    for j in range(1, chips):
        pl.semaphore_signal(
            barrier,
            inc=1,
            device_id={"face": ((chip + j) % chips) * 2 + core},
            device_id_type=MESH,
        )
    for j in range(1, members):
        pl.semaphore_signal(
            barrier, inc=1, device_id={"member": (member + j) % members}, device_id_type=MESH
        )
    return lambda: pl.semaphore_wait(barrier, chips + members - 1)


class FaceGather:
    def __init__(self, at, chips, sems):
        self.at, self.chips, self.sems = at, chips, sems
        face = lax.axis_index("face")
        self.face, self.core, self.chip = face, face % 2, face // 2
        self.partner = self.chip * 2 + 1 - self.core

    def direct(self, j):
        mine = self.at(self.face, None)
        return rcopy(
            mine,
            mine,
            self.sems.at[0, j],
            self.sems.at[1, j],
            face=((self.chip + j) % self.chips) * 2 + self.core,
        )

    def forward(self, j):
        block = self.at(((self.chip + self.chips - j) % self.chips) * 2 + self.core, None)
        return rcopy(block, block, self.sems.at[2, j], self.sems.at[3, j], face=self.partner)

    def start(self):
        for j in range(1, self.chips):
            self.direct(j).start()
        self.forward(0).start()

    def relay_first(self):
        pass

    def relay_rest(self):
        for j in range(1, self.chips):
            self.direct(j).wait_recv()
            self.forward(j).start()

    def finish(self):
        for j in range(1, self.chips):
            self.direct(j).wait_send()
        for j in range(self.chips):
            self.forward(j).wait()


class SquareGather:
    def __init__(self, at, chips, sems):
        self.at, self.sems = at, sems
        face = lax.axis_index("face")
        core, chip = face % 2, face // 2
        col, row = chip % 2, chip // 2
        self.face = face
        self.partner = chip * 2 + 1 - core
        self.beside = (row * 2 + 1 - col) * 2 + core
        self.below = ((1 - row) * 2 + col) * 2 + core
        self.across = ((1 - row) * 2 + 1 - col) * 2 + core

    def direct(self, k):
        to = (self.beside, self.beside, self.below, self.below, self.below, self.beside)[k]
        block = (self.face,) * 4 + (self.beside, self.below)
        ref = self.at(block[k], (0, 1, 1, 0, 0, 1)[k])
        return rcopy(ref, ref, self.sems.at[0, k], self.sems.at[1, k], face=to)

    def forward(self, k):
        if k == 6:
            ref = self.at(self.face, None)
        else:
            block = (
                self.beside,
                self.beside,
                self.below,
                self.below,
                self.across,
                self.across,
            )
            ref = self.at(block[k], (0, 1, 1, 0, 0, 1)[k])
        return rcopy(ref, ref, self.sems.at[2, k], self.sems.at[3, k], face=self.partner)

    def start(self):
        for k in (0, 2, 1, 3):
            self.direct(k).start()
        self.forward(6).start()

    def relay_first(self):
        for k, onward in ((0, 4), (2, 5)):
            self.direct(k).wait_recv()
            self.direct(onward).start()
            self.forward(k).start()

    def relay_rest(self):
        for k in (1, 3, 4, 5):
            self.direct(k).wait_recv()
            self.forward(k).start()

    def finish(self):
        for k in range(6):
            self.direct(k).wait_send()
        for k in range(7):
            self.forward(k).wait()


def units(ref, rows, start, count):
    if len(ref.shape) == 3:
        return ref.at[pl.ds(start, count)] if count > 1 else ref.at[start]
    return ref.at[pl.ds(pl.multiple_of(start * rows, rows), count * rows)]


def gather_rows(ref, rows, members, chips, sems):
    def at(block, part):
        if part is None:
            return units(ref, rows, block * members, members)
        half = members // 2
        return units(ref, rows, block * members + part * half, half)

    return (SquareGather if chips == 4 and members % 2 == 0 else FaceGather)(at, chips, sems)


def gather_edges(ref, start, count, chips, sems):
    def at(block, part):
        if part is None:
            return ref.at[block, pl.ds(start, count)]
        half = count // 2
        return ref.at[block, pl.ds(start + part * half, half)]

    return (SquareGather if chips == 4 and count % 2 == 0 else FaceGather)(at, chips, sems)


class LineGather:
    def __init__(self, src, ref, rows, members, sems):
        self.src, self.ref, self.rows, self.members, self.sems = src, ref, rows, members, sems
        self.face, self.member = lax.axis_index("face"), lax.axis_index("member")

    def at(self, member):
        return units(self.ref, self.rows, self.face * self.members + member, 1)

    def own(self):
        return pltpu.make_async_copy(self.src, self.at(self.member), self.sems.at[0, 0])

    def send(self, j):
        to = (self.member + j) % self.members
        return rcopy(
            self.src, self.at(self.member), self.sems.at[0, j], self.sems.at[1, j], member=to
        )

    def came(self, j):
        origin = (self.member + self.members - j) % self.members
        return rcopy(
            self.src, self.at(origin), self.sems.at[0, j], self.sems.at[1, j], member=origin
        )

    def start(self):
        self.own().start()
        for j in range(1, self.members):
            self.send(j).start()

    def wait(self):
        self.own().wait()
        for j in range(1, self.members):
            self.came(j).wait_recv()
            self.send(j).wait_send()


class PlaneLine:
    def __init__(self, src, ref, chips, members, sems):
        self.src, self.ref, self.chips, self.members, self.sems = src, ref, chips, members, sems
        self.member = lax.axis_index("member")
        face = lax.axis_index("face")
        self.core, self.chip = face % 2, face // 2
        self.partner = self.chip * 2 + 1 - self.core

    def mine(self):
        return self.ref.at[(self.member * 2 + self.core) * self.chips + self.chip]

    def own(self):
        return pltpu.make_async_copy(self.src, self.mine(), self.sems.at[0, 0])

    def plane(self, j):
        to = ((self.chip + j) % self.chips) * 2 + self.core
        return rcopy(self.src, self.mine(), self.sems.at[0, j], self.sems.at[1, j], face=to)

    def group(self, j):
        member = (self.member + self.members - j) % self.members
        return self.ref.at[pl.ds((member * 2 + self.core) * self.chips, self.chips)]

    def line(self, j):
        to = (self.member + j) % self.members
        ref = self.group(0)
        return rcopy(ref, ref, self.sems.at[2, j], self.sems.at[3, j], member=to)

    def cross(self, j):
        ref = self.group(j)
        return rcopy(ref, ref, self.sems.at[4, j], self.sems.at[5, j], face=self.partner)

    def start(self):
        self.own().start()
        for j in range(1, self.chips):
            self.plane(j).start()

    def relay_first(self):
        self.own().wait()
        for j in range(1, self.chips):
            self.plane(j).wait_recv()
        for j in range(1, self.members):
            self.line(j).start()
        self.cross(0).start()

    def relay_rest(self):
        for j in range(1, self.members):
            self.line(j).wait_recv()
            self.cross(j).start()

    def finish(self):
        for j in range(1, self.chips):
            self.plane(j).wait_send()
        for j in range(1, self.members):
            self.line(j).wait_send()
        for j in range(self.members):
            self.cross(j).wait()


def coded(v):
    axes = tuple(range(v.ndim - 1))
    most = jnp.max(jnp.abs(v), axis=axes, keepdims=True)
    code = jnp.round(v * (TOP / jnp.maximum(most, 1e-33))).astype(jnp.int32).astype(i16)
    most = most.reshape(1, v.shape[-1])
    return code, jnp.broadcast_to(most * (1.0 / TOP), (8, v.shape[-1]))


def decoded(code, scale):
    return code.astype(jnp.int32).astype(f32) * scale[0:1, :]


class Scatter:
    def __init__(self, g, chips, members, scratch, sems):
        self.g, self.chips, self.members = g, chips, members
        self.fromcore, self.acc, self.out1, self.in1, self.out2, self.in2 = scratch[:6]
        self.sc = scratch[6:]
        self.sems = sems
        face = lax.axis_index("face")
        self.member = lax.axis_index("member")
        self.core, self.chip = face % 2, face // 2
        self.partner = self.chip * 2 + 1 - self.core
        self.order = list(range(1, chips)) + [0]

    def part(self, chip, core):
        return pl.ds((chip * 2 + core) * self.members, self.members)

    def there(self, j):
        return (self.chip + j) % self.chips

    def core_copy(self, j):
        return rcopy(
            self.g.at[self.part(self.there(j), 1 - self.core)],
            self.fromcore.at[j],
            self.sems.at[0, j],
            self.sems.at[1, j],
            face=self.partner,
        )

    def copies(self, first, boxes, j, **to):
        s = self.sems
        return [
            rcopy(a.at[j], b.at[j], s.at[i, j], s.at[i + 1, j], **to)
            for i, (a, b) in zip((first, first + 2), boxes)
        ]

    def chip_copies(self, j):
        boxes = [(self.out1, self.in1)] + ([(self.sc[0], self.sc[1])] if self.sc else [])
        return self.copies(2, boxes, j, face=self.there(j) * 2 + self.core)

    def line_copies(self, j):
        boxes = [(self.out2, self.in2)] + ([(self.sc[2], self.sc[3])] if self.sc else [])
        return self.copies(6, boxes, j, member=(self.member + j) % self.members)

    def core_start(self):
        for j in self.order:
            self.core_copy(j).start()

    def core_done(self):
        for j in self.order:
            self.core_copy(j).wait_recv()
            total = self.g[self.part(self.there(j), self.core)] + self.fromcore[j]
            if j == 0:
                self.acc[...] = total
                continue
            if self.sc:
                self.out1[j], self.sc[0][j] = coded(total)
            else:
                self.out1[j] = total
            for c in self.chip_copies(j):
                c.start()

    def summed(self, to):
        v = self.acc[to]
        for i in range(1, self.chips):
            piece = self.in1[i, to]
            v = v + (decoded(piece, self.sc[1][i]) if self.sc else piece)
        return v

    def chip_done(self):
        for j in range(1, self.chips):
            for c in self.chip_copies(j):
                c.wait_recv()
        for j in range(1, self.members):
            v = self.summed((self.member + j) % self.members)
            if self.sc:
                self.out2[j], self.sc[2][j] = coded(v)
            else:
                self.out2[j] = v
            for c in self.line_copies(j):
                c.start()

    def line_done(self):
        total = self.summed(self.member)
        for j in range(1, self.members):
            for c in self.line_copies(j):
                c.wait_recv()
            piece = self.in2[j]
            total = total + (decoded(piece, self.sc[3][j]) if self.sc else piece)
        return total

    def finish(self):
        for j in range(self.chips):
            self.core_copy(j).wait_send()
        for j in range(1, self.chips):
            for c in self.chip_copies(j):
                c.wait_send()
        for j in range(1, self.members):
            for c in self.line_copies(j):
                c.wait_send()


def scatter_scratch(chips, members, rows, lanes, code):
    kind = i16 if code else f32
    out = [
        VMEM((chips, members, rows, lanes), f32),
        VMEM((members, rows, lanes), f32),
        VMEM((chips, members, rows, lanes), kind),
        VMEM((chips, members, rows, lanes), kind),
        VMEM((members, rows, lanes), kind),
        VMEM((members, rows, lanes), kind),
    ]
    if code:
        out += [VMEM((chips, 8, lanes), f32)] * 2 + [VMEM((members, 8, lanes), f32)] * 2
    return out


def put_rows(ref, first, v):
    rows, done = ref.shape[1], 0
    while done < v.shape[0]:
        block, at = divmod(first + done, rows)
        size = min(rows - at, v.shape[0] - done)
        ref[block, at : at + size, :] = v[done : done + size]
        done += size


def sides_of(field):
    h, w, c = field.shape
    return [
        field[0],
        field[:, w - 1 : w, :].reshape(h, c),
        field[h - 1],
        field[:, 0:1, :].reshape(h, c),
    ]


def g_of(v):
    return v * lax.rsqrt(v * v + smooth_sq)


class Step:
    def __init__(self, dims, refs):
        self.__dict__.update(dims)
        self.__dict__.update(refs)
        face = lax.axis_index("face")
        self.face, self.member = face, lax.axis_index("member")


    def tables(self):
        first = self.face * self.T
        total = self.place.shape[0]

        def fill(i, carry):
            tile = self.place[first + i]
            for a in range(4):
                want = self.glue[0, a, tile]

                def look(s, slot):
                    return jnp.where(self.place[s] == want, s, slot)

                slot = lax.fori_loop(0, total, look, jnp.int32(0), unroll=8)
                owner = slot // self.T
                self.at_face[i * 4 + a] = owner
                self.at_slot[i * 4 + a] = slot - owner * self.T
                self.at_side[i * 4 + a] = self.glue[1, a, tile]
            size = 4 * self.w
            row = lax.broadcasted_iota(jnp.int32, (size, size), 0)
            col = lax.broadcasted_iota(jnp.int32, (size, size), 1)
            side = row // self.w
            at = row - side * self.w
            flag = jnp.zeros((size, size), jnp.int32)
            for a in range(4):
                flag = jnp.where(side == a, self.glue[2, a, tile], flag)
            target = side * self.w + jnp.where(flag == 1, self.w - 1 - at, at)
            self.turn[i] = jnp.where(col == target, 1.0, 0.0).astype(bf16)
            return carry

        lax.fori_loop(0, self.T, fill, 0)

    def rims_from(self, box, m):
        def one(i, carry):
            cat = jnp.concatenate(
                [
                    box[self.at_face[i * 4 + a], self.at_slot[i * 4 + a] * 4 + self.at_side[i * 4 + a]]
                    for a in range(4)
                ],
                axis=0,
            )
            self.rims[m * self.T + i] = mm(self.turn[i], cat)
            return carry

        lax.fori_loop(0, self.T, one, 0, unroll=True)

    def turn_inputs(self):
        for p in range(self.P):
            o = [self.obs[p * self.G + g].astype(f32).T for g in range(self.G)]
            self.obs_wide[p] = jnp.concatenate(o, axis=1) if self.G > 1 else o[0]

    def cut(self, box, i):
        for a, v in enumerate(sides_of(self.field)):
            box[self.face, i * 4 + a] = v.astype(bf16)

    def cut_input(self, m):
        def one(i, carry):
            v = self.x[m * self.T + i].astype(f32)
            self.field[...] = v.reshape(self.h, self.w, self.c)
            self.cut(self.edges_x[m], i)
            return carry

        lax.fori_loop(0, self.T, one, 0)


    def conv(self, u, src, x3, w_ref, slope):
        h, w, c, G = self.h, self.w, self.c, self.G
        k0 = u * G
        pad = self.pad
        for g in range(G):
            k = k0 + g
            rims = self.rims[k]
            pad[1 : h + 1, 8 : 8 + w, :] = src[k].reshape(h, w, c).astype(f32)
            pad[0, 8 : 8 + w, :] = rims[0:w]
            pad[1 : h + 1, 8 + w : 9 + w, :] = rims[w : w + h].reshape(h, 1, c)
            pad[h + 1, 8 : 8 + w, :] = rims[w + h : 2 * w + h]
            pad[1 : h + 1, 7:8, :] = rims[2 * w + h :].reshape(h, 1, c)
            for b in range(3):
                x3[k, :, :, b * c : (b + 1) * c] = pad[:, 7 + b : 7 + b + w, :].astype(bf16)
        pre = None
        for a in range(3):
            part = mm(
                x3[pl.ds(k0, G), a : a + h].reshape(G * h * w, 3 * c),
                w_ref[3 * a * c : 3 * (a + 1) * c, :],
            )
            pre = part if pre is None else pre + part
        s = 1.0 / (1.0 + jnp.exp(-pre))
        act = pre * s
        slope[pl.ds(k0, G)] = (s + act * (1.0 - s)).reshape(G, h * w, c)
        return act.astype(bf16)

    def conv_first(self, u):
        act = self.conv(u, self.x, self.x3_one, self.w1, self.d_one)
        cells = self.h * self.w
        for g in range(self.G):
            self.act_one[u * self.G + g] = act[g * cells : (g + 1) * cells]

    def cut_act(self, m):
        h, w, c = self.h, self.w, self.c

        def one(i, carry):
            self.field[...] = self.act_one[m * self.T + i].astype(f32).reshape(h, w, c)
            self.cut(self.edges_a[m], i)
            return carry

        lax.fori_loop(0, self.T, one, 0)

    def go(self, u, j):
        to = (self.member + j) % self.Z
        return rcopy(
            self.packed.at[u, to],
            self.came.at[u, j],
            self.ssem.at[0, u, j],
            self.ssem.at[1, u, j],
            member=to,
        )

    def home(self, i, j, here=False):
        back = (self.member + j) % self.Z if here else self.member
        return rcopy(
            self.slopes.at[i, j],
            self.back.at[i, back],
            self.ssem.at[2, i, j],
            self.ssem.at[3, i, j],
            member=(self.member + self.Z - j) % self.Z,
        )

    def conv_last(self, u):
        act = self.conv(u, self.act_one, self.x3_two, self.w2, self.d_two)
        G, cells, part = self.G, self.h * self.w, self.part
        outs = []
        for g in range(G):
            own = act[g * cells : (g + 1) * cells]
            self.act_two[u * G + g] = own
            outs.append(mm(self.head_t[0 : self.V, :], own, NT).astype(bf16))
        for q in range(self.Z):
            cols = [o[:, q * part : (q + 1) * part] for o in outs]
            self.packed[u, q] = jnp.concatenate(cols, axis=1) if G > 1 else cols[0]
        for j in range(1, self.Z):
            self.go(u, j).start()


    def score(self, p):
        ensemble = self.H * self.Z
        for m in range(self.H):
            for j in range(1, self.Z):
                self.go(m * self.P + p, j).wait_recv()
        rows = 16 if self.V % 16 == 0 else self.V
        for r in range(0, self.V, rows):
            at = slice(r, r + rows)
            o = self.obs_wide[p, at, :]
            names = [(m, j) for j in range(self.Z) for m in range(self.H)]
            vals = []
            for m, j in names:
                u = m * self.P + p
                v = self.packed[u, self.member, at, :] if j == 0 else self.came[u, j, at, :]
                vals.append(v.astype(f32))
            paired = [None] * len(vals)
            for a in range(len(vals)):
                for b in range(a + 1, len(vals)):
                    t = g_of(vals[a] - vals[b])
                    paired[a] = t if paired[a] is None else paired[a] + t
                    paired[b] = -t if paired[b] is None else paired[b] - t
            for (m, j), v, t in zip(names, vals, paired):
                i = p * self.H + m
                s = (g_of(v - o) / ensemble - t / (ensemble * ensemble)) / self.h
                if j == 0:
                    self.back[i, self.member, at, :] = s.astype(bf16)
                else:
                    self.slopes[i, j, at, :] = s.astype(bf16)
        for m in range(self.H):
            for j in range(1, self.Z):
                self.home(p * self.H + m, j).start()


    def prepare_back(self):
        c = self.c
        for a in range(3):
            for b in range(3):
                tap = self.w2[(3 * a + b) * c : (3 * a + b + 1) * c, :]
                self.va[a, :, b * c : (b + 1) * c] = tap
                if b == 0:
                    self.vb[0, :, a * c : (a + 1) * c] = tap
                if b == 2:
                    self.vb[1, :, a * c : (a + 1) * c] = tap
        self.hg[...] = jnp.zeros_like(self.hg)
        self.pad2[...] = jnp.zeros_like(self.pad2)

    def lanes(self, k):
        cells = self.h * self.w
        return pl.ds(pl.multiple_of(k * cells, cells), cells)

    def backward(self, i):
        h, w, c, G, H, part = self.h, self.w, self.c, self.G, self.H, self.part
        p = i // H
        m = i - p * H
        u = m * self.P + p
        for j in range(1, self.Z):
            self.home(i, j, here=True).wait_recv()
        pad = self.pad2
        for g in range(G):
            k = u * G + g
            slope_out = jnp.concatenate(
                [self.back[i, q][:, g * part : (g + 1) * part] for q in range(self.Z)], axis=1
            )
            self.hg[0 : self.V, :] += mm(slope_out, self.act_two[k])
            back = mm(slope_out, self.head_t[0 : self.V, :], TN)
            slope = (back * self.d_two[k]).astype(bf16)
            self.turned[:, self.lanes(k)] = slope.T
            pad[2 : h + 2, 8 : 8 + w, :] = slope.astype(f32).reshape(h, w, c)
            for b in range(3):
                self.s3[g, :, :, b * c : (b + 1) * c] = pad[:, 9 - b : 9 - b + w, :].astype(bf16)
            left = pad[:, 8:9, :].reshape(h + 4, c)
            right = pad[:, 7 + w : 8 + w, :].reshape(h + 4, c)
            for a in range(3):
                self.cols[0, g, :, a * c : (a + 1) * c] = left[3 - a : 3 - a + h].astype(bf16)
                self.cols[1, g, :, a * c : (a + 1) * c] = right[3 - a : 3 - a + h].astype(bf16)
        full = None
        for a in range(3):
            lhs = self.s3[:, 2 - a : 4 - a + h].reshape(G * (h + 2) * w, 3 * c)
            one = mm(lhs, self.va[a], NT)
            full = one if full is None else full + one
        full = full.reshape(G, h + 2, w, c).astype(bf16)
        self.inner[pl.ds(u * G, G)] = full[:, 1 : h + 1]
        lefts = mm(self.cols[0].reshape(G * h, 3 * c), self.vb[0], NT).astype(bf16)
        rights = mm(self.cols[1].reshape(G * h, 3 * c), self.vb[1], NT).astype(bf16)
        for g in range(G):
            at = (i * G + g) * 4
            sides = (
                full[g, 0],
                rights[g * h : (g + 1) * h],
                full[g, h + 1],
                lefts[g * h : (g + 1) * h],
            )
            for a in range(4):
                self.borders[self.face, at + a] = sides[a]

    def rims_back(self, m):
        G = self.G

        def one(i, carry):
            sides = []
            for a in range(4):
                at = i * 4 + a
                slot = self.at_slot[at]
                unit = slot // G
                j = (m * G + slot - unit * G) * 4 + self.at_side[at]
                sides.append(self.borders[self.at_face[at], unit * (self.H * G * 4) + j])
            self.rims[m * self.T + i] = mm(self.turn[i], jnp.concatenate(sides, axis=0))
            return carry

        lax.fori_loop(0, self.T, one, 0, unroll=True)

    def slope_first(self, k):
        h, w, c = self.h, self.w, self.c
        rims, field = self.rims[k], self.field
        field[...] = self.inner[k].astype(f32)
        field[0] += rims[0:w]
        field[:, w - 1 : w, :] += rims[w : w + h].reshape(h, 1, c)
        field[h - 1] += rims[w + h : 2 * w + h]
        field[:, 0:1, :] += rims[2 * w + h :].reshape(h, 1, c)
        slope = (field[...].reshape(h * w, c) * self.d_one[k]).astype(bf16)
        self.turned[:, self.lanes(k)] = slope.T

    def products(self, kb, x3, cols):
        h, w, c, K = self.h, self.w, self.c, self.K
        cells = h * w
        at = pl.ds(pl.multiple_of(kb * K * cells, K * cells), K * cells)
        for a in range(3):
            rhs = x3[pl.ds(kb * K, K), a : a + h].reshape(K * cells, 3 * c)
            self.acc[a, cols, :] += mm(self.turned[cols, at], rhs)

    def turn_out(self, ref, cols):
        c = self.c
        for a in range(3):
            for b in range(3):
                put_rows(ref, (3 * a + b) * c, self.acc[a, cols, b * c : (b + 1) * c].T)


def hooked(steps, body, before=None, after=None):
    before, after = before or {}, after or {}

    def one(i, carry):
        for s, todo in sorted(before.items()):
            pl.when(i == s)(todo)
        body(i)
        for s, todo in sorted(after.items()):
            pl.when(i == s)(todo)
        return carry

    lax.fori_loop(0, steps, one, 0)


def merge(*items):
    out = {}
    for at, todo in items:
        out.setdefault(at, []).append(todo)

    def run(todos):
        def go():
            for t in todos:
                t()

        return go

    return {at: run(todos) for at, todos in out.items()}


def step_kernel(dims, names, *refs):
    s = Step(dims, dict(zip(names, refs)))
    chips, members, H, PU = s.chips, s.Z, s.H, s.P
    gsem = s.gsem
    s.edges_x = [getattr(s, f"edges_x{m}") for m in range(H)]
    s.edges_a = [getattr(s, f"edges_a{m}") for m in range(H)]
    w1 = s.w1_apart if hasattr(s, "w1_apart") else s.w1

    def settle():
        if hasattr(s, "w1_apart"):
            for d in range(chips * 2 * members):
                s.w1[d * s.rows : (d + 1) * s.rows, :] = s.w1_apart[d]

    def settle_last():
        for d in range(chips * 2 * members):
            face, member = divmod(d, members)
            at = (member * 2 + face % 2) * chips + face // 2
            s.w2[d * s.rows : (d + 1) * s.rows, :] = s.w2_apart[at]
            s.heads[d * s.hrows : (d + 1) * s.hrows, :] = s.heads_apart[at]

    lw1 = LineGather(s.w_own.at[0], w1, s.rows, members, s.lsem.at[0])
    gw1 = gather_rows(w1, s.rows, members, chips, gsem.at[0])
    later = [
        PlaneLine(s.w_own.at[1], s.w2_apart, chips, members, s.psem.at[0]),
        PlaneLine(s.head_own, s.heads_apart, chips, members, s.psem.at[1]),
    ]
    sides, share = s.T * 4, H * s.G * 4
    gx = [gather_edges(s.edges_x[m], 0, sides, chips, gsem.at[3 + m]) for m in range(H)]
    ga = [gather_edges(s.edges_a[m], 0, sides, chips, gsem.at[3 + H + m]) for m in range(H)]
    gb = [
        gather_edges(s.borders, p * share, share, chips, gsem.at[3 + 2 * H + p])
        for p in range(PU)
    ]

    all_here = greet(chips, members)
    for layer in range(2):
        s.w_own[layer] = s.weights[:, layer, :]
    s.head_own[...] = jnp.zeros_like(s.head_own)
    s.head_own[:, 0 : s.V] = s.head[...]
    s.cut_input(0)
    all_here()
    lw1.start()
    gx[0].start()
    for m in range(1, H):
        s.cut_input(m)
    s.pad[...] = jnp.zeros_like(s.pad)
    lw1.wait()
    gw1.start()
    for g in later:
        g.start()
    s.tables()
    s.turn_inputs()
    gx[0].relay_first()
    gw1.relay_first()
    for g in later:
        g.relay_first()
    gx[0].relay_rest()
    gw1.relay_rest()
    for m in range(1, H):
        gx[m].start()
    gw1.finish()
    settle()

    last = H * PU - 1

    def ready_x(m):
        gx[m].finish()
        s.rims_from(s.edges_x[m], m)

    def send_a(m):
        s.cut_act(m)
        ga[m].start()

    def ready_a(m):
        ga[m].finish()
        s.rims_from(s.edges_a[m], m)

    before = {m * PU: functools.partial(ready_x, m) for m in range(H)}
    after = []
    for m in range(1, H):
        at = m * PU - 1
        after.append((max(at - 1, 0), gx[m].relay_first))
        after.append((at, functools.partial(send_a, m - 1)))
        after.append((at, gx[m].relay_rest))
        after.append((at, ga[m - 1].relay_first))
    hooked(H * PU, s.conv_first, before, merge(*after))
    s.cut_act(H - 1)
    ga[H - 1].start()
    for m in range(H - 1):
        ga[m].relay_rest()
    for g in later:
        g.relay_rest()
    for g in later:
        g.finish()
    settle_last()
    s.head_t[...] = s.heads[...].astype(f32).T.astype(bf16)

    before = {m * PU: functools.partial(ready_a, m) for m in range(H)}
    after = [
        (max((H - 1) * PU - 3, 0), ga[H - 1].relay_first),
        (max((H - 1) * PU - 1, 0), ga[H - 1].relay_rest),
    ]
    hooked(H * PU, s.conv_last, before, merge(*after))
    s.prepare_back()

    lax.fori_loop(0, PU, lambda p, carry: (s.score(p), carry)[1], 0)
    after = []
    late = []
    total = H * PU
    for p in range(PU):
        at = (p + 1) * H - 1
        after.append((at, gb[p].start))
        for step, todo in ((at + 2, gb[p].relay_first), (at + 4, gb[p].relay_rest)):
            if step < total:
                after.append((step, todo))
            else:
                late.append((min(step - total, s.n // s.K - 1), todo))
    hooked(total, s.backward, None, merge(*after))

    s.acc[...] = jnp.zeros_like(s.acc)
    hooked(s.n // s.K, lambda kb: s.products(kb, s.x3_two, slice(0, s.c)), None, merge(*late))
    s_two = Scatter(s.two, chips, members, [getattr(s, f"t{i}") for i in range(10)], s.csem.at[0])
    s_head = Scatter(s.hg_t, chips, members, [getattr(s, f"h{i}") for i in range(6)], s.csem.at[1])
    s_one = [
        Scatter(
            getattr(s, f"one{q}"),
            chips,
            members,
            [getattr(s, f"o{q}{i}") for i in range(10)],
            s.csem.at[2 + q],
        )
        for q in range(s.cuts)
    ]
    s.turn_out(s.two, slice(0, s.c))
    s.acc[...] = jnp.zeros_like(s.acc)
    put_rows(s.hg_t, 0, s.hg[...].T)
    s_two.core_start()
    s_head.core_start()

    for p in range(PU):
        gb[p].finish()
    for m in range(H):
        s.rims_back(m)
    s_two.core_done()
    s_head.core_done()
    lax.fori_loop(0, s.n, lambda k, carry: (s.slope_first(k), carry)[1], 0)
    wide = s.c // s.cuts
    cols = [slice(q * wide, (q + 1) * wide) for q in range(s.cuts)]
    for q in range(s.cuts):
        after = {0: s_one[q - 1].core_done} if q else None
        body = functools.partial(lambda at, kb: s.products(kb, s.x3_one, at), cols[q])
        hooked(s.n // s.K, body, None, after)
        s.turn_out(getattr(s, f"one{q}"), cols[q])
        s_one[q].core_start()
    s_two.chip_done()
    s_head.chip_done()
    s_one[-1].core_done()
    for q in range(s.cuts - 1):
        s_one[q].chip_done()
    s.grads[:, 1, :] = s_two.line_done()
    s.head_out[...] = s_head.line_done()
    s_one[-1].chip_done()
    for q in range(s.cuts):
        s.grads[:, 0, cols[q]] = s_one[q].line_done()
    for scatter in [s_two, s_head] + s_one:
        scatter.finish()
    for u in range(H * PU):
        for j in range(1, members):
            s.go(u, j).wait_send()
            s.home(u, j).wait_send()


def shards(faces, zs, features, observed, conv_weights, head_weight, adjacency, placement_map):
    H, T, h, w, c = features.shape
    n = H * T
    V = head_weight.shape[1]
    rows, hrows = conv_weights.shape[0], head_weight.shape[0]
    lanes = -(-V // 128) * 128
    chips = faces // 2
    G = 2 if T % 2 == 0 else 1
    PU = T // G
    K = 6 if n % 6 == 0 else (2 if n % 2 == 0 else 1)
    part = observed.shape[-1]
    cells = h * w
    cuts = 2 if c % 256 == 0 else 1
    dims = dict(
        H=H, T=T, h=h, w=w, c=c, n=n, V=V, rows=rows, hrows=hrows, chips=chips, Z=zs, G=G, P=PU,
        K=K, part=part, cuts=cuts,
    )
    side = 4 * w
    total_rows = rows * faces * zs
    total_heads = hrows * faces * zs
    scratch = {
        "at_face": SMEM((T * 4,), jnp.int32),
        "at_slot": SMEM((T * 4,), jnp.int32),
        "at_side": SMEM((T * 4,), jnp.int32),
        "turn": VMEM((T, side, side), bf16),
        "obs_wide": VMEM((PU, V, G * part), f32),
        "w_own": VMEM((2, rows, c), bf16),
        "rims": VMEM((n, side, c), f32),
        "field": VMEM((h, w, c), f32),
        "pad": VMEM((h + 2, w + 16, c), f32),
        "pad2": VMEM((h + 4, w + 16, c), f32),
        "head_own": VMEM((hrows, lanes), bf16),
        "w1": VMEM((total_rows, c), bf16),
        "w2": VMEM((total_rows, c), bf16),
        "heads": VMEM((total_heads, lanes), bf16),
        "head_t": VMEM((lanes, total_heads), bf16),
        "x3_one": VMEM((n, h + 2, w, 3 * c), bf16),
        "x3_two": VMEM((n, h + 2, w, 3 * c), bf16),
        "d_one": VMEM((n, cells, c), f32),
        "d_two": VMEM((n, cells, c), f32),
        "act_one": VMEM((n, cells, c), bf16),
        "act_two": VMEM((n, cells, c), bf16),
        "packed": VMEM((H * PU, zs, V, G * part), bf16),
        "came": VMEM((H * PU, zs, V, G * part), bf16),
        "slopes": VMEM((H * PU, zs, V, G * part), bf16),
        "back": VMEM((H * PU, zs, V, G * part), bf16),
        "va": VMEM((3, c, 3 * c), bf16),
        "vb": VMEM((2, c, 3 * c), bf16),
        "s3": VMEM((G, h + 4, w, 3 * c), bf16),
        "cols": VMEM((2, G, h, 3 * c), bf16),
        "inner": VMEM((n, h, w, c), bf16),
        "turned": VMEM((c, n * cells), bf16),
        "acc": VMEM((3, c, 3 * c), f32),
        "hg": VMEM((lanes, c), f32),
        "hg_t": VMEM((faces * zs, hrows, lanes), f32),
        "two": VMEM((faces * zs, rows, c), f32),
        "borders": VMEM((faces, PU * H * G * 4, w, c), bf16),
    }
    for m in range(H):
        scratch[f"edges_x{m}"] = VMEM((faces, T * 4, w, c), bf16)
        scratch[f"edges_a{m}"] = VMEM((faces, T * 4, w, c), bf16)
    sums = [("t", rows, c, True), ("h", hrows, lanes, False)]
    for q in range(cuts):
        scratch[f"one{q}"] = VMEM((faces * zs, rows, c // cuts), f32)
        sums.append((f"o{q}", rows, c // cuts, True))
    for name, r, lane, code in sums:
        for i, v in enumerate(scatter_scratch(chips, zs, r, lane, code)):
            scratch[f"{name}{i}"] = v
    scratch["w2_apart"] = VMEM((faces * zs, rows, c), bf16)
    scratch["heads_apart"] = VMEM((faces * zs, hrows, lanes), bf16)
    if rows % 16:
        scratch["w1_apart"] = VMEM((faces * zs, rows, c), bf16)
    dma = pltpu.SemaphoreType.DMA
    scratch["gsem"] = dma((3 + 2 * H + PU, 4, chips + 3))
    scratch["lsem"] = dma((1, 2, zs))
    scratch["psem"] = dma((2, 6, max(chips, zs)))
    scratch["ssem"] = dma((4, H * PU, zs))
    scratch["csem"] = dma((2 + cuts, 10, max(chips, zs)))
    vmem = pl.BlockSpec(memory_space=VMEM)
    smem = pl.BlockSpec(memory_space=SMEM)
    ins = ["place", "glue", "x", "obs", "weights", "head"]
    outs = ["grads", "head_out"]
    grads, head_out = pl.pallas_call(
        functools.partial(step_kernel, dims, ins + outs + list(scratch)),
        out_shape=[
            jax.ShapeDtypeStruct((rows, 2, c), f32),
            jax.ShapeDtypeStruct((hrows, lanes), f32),
        ],
        in_specs=[smem, smem] + [vmem] * 4,
        out_specs=[vmem] * 2,
        scratch_shapes=list(scratch.values()),
        compiler_params=pltpu.CompilerParams(
            collective_id=1, has_side_effects=True, vmem_limit_bytes=LIMIT
        ),
        name="step",
    )(
        placement_map,
        adjacency.transpose(2, 1, 0),
        features.reshape(n, cells, c),
        observed.transpose(0, 2, 1),
        conv_weights,
        head_weight,
    )
    return grads, head_out[:, :V]


def solution(mesh):
    in_specs = (
        P("member", "face", None, None, None),
        P("face", None, "member"),
        P(("face", "member"), None, None),
        P(("face", "member"), None),
        P(),
        P(),
    )
    out_specs = (P(("face", "member"), None, None), P(("face", "member"), None))
    body = functools.partial(shards, mesh.shape["face"], mesh.shape["member"])
    return jax.shard_map(body, mesh=mesh, in_specs=in_specs, out_specs=out_specs, check_vma=False)
```
